128 devices in a mesh: row: 16 (over y, x_lo, core), col: 8 (over z, x_hi).
Axes of the slice: x: 4 (x_hi: 2, x_lo: 2; x = x_hi * 2 + x_lo), y: 4, z: 4, core: 2. Of those that a mesh axis runs over, the one named last changes fastest.
Arguments:
- schur_rows: float32 [1024, 1024], P('row', 'col'), may hold values from -0.40335507 to 0.40335507
- inverses: float32 [1024, 64, 2048], P('row', None, 'col'), may hold values from -0.75 to 0.75
- coupling: float32 [1024, 2048], P('row'), may hold values from -6 to 6
- selected: int32 [2048], P('col'), may hold values from 0 to 2047, each once
- schur_basis: bfloat16 [49152, 1024], P('row', 'col'), may hold values from -0.1875 to 0.1875
Outputs:
- eigenvectors: bfloat16 [49152, 2048], P('row', 'col')
- solved_slab: float32 [1024, 2048], P('row', 'col')
The draws below stay inside these ranges and needn't reach their ends.
Inputs may be any that keep to these rules, and one draw needn't show every extreme that they name: `selected`: each of the 2048 indices appears exactly once.
All inputs are finite; a program needn't handle non-finite values.
Results may differ from the reference program's by a relative error of at most 0.0049.
Values may be sent and summed in bfloat16 or wider, within the bound.
No kernel may reach another device: no remote copies, remote signals or barrier semaphores. Data moves between devices by JAX's collectives and lax.ppermute only.
A program may use at most 64 MiB of HBM per device.

```python
import jax
import jax.numpy as jnp
from jax import lax

NB = 64
W = 1024
K = 2048
ROWS = 49152


def draw_schur_rows(key, part):
    folded = jax.random.fold_in(key, 7)
    tile_index = jnp.arange(W) // NB
    distance = tile_index[None, :] - tile_index[:, None]
    values = jnp.clip(jax.random.normal(folded, (W, W), jnp.float32), -3.5, 3.5)
    near_spread = (0.85 / NB) ** 0.5
    far_spread = 0.08 / NB ** 0.5
    other_spread = 0.25 / NB ** 0.5
    spread = jnp.where(distance == 1, near_spread, jnp.where(distance > 1, far_spread, other_spread))
    return (values * spread).astype(jnp.float32)


def steps_of(own_key, extent, pieces, least, largest):
    level, own = 1.0, jax.random.fold_in(own_key, 6)
    for position, blocks in pieces:
        draws = jnp.exp(jax.random.uniform(jax.random.fold_in(own, position), (blocks,), jnp.float32, least / len(pieces), largest / len(pieces)))
        level = level * jnp.repeat(draws, extent[position] // blocks).reshape([-1 if axis == position else 1 for axis in range(len(extent))])
    return level


def noise(key, extent, deviation, bound, cuts=(), kind=jnp.bfloat16):
    drawn = deviation * jax.random.normal(key, extent, jnp.float32)
    if cuts:
        drawn = drawn * steps_of(key, extent, cuts, -0.22, 0.18)
    return jnp.clip(drawn, -bound, bound).astype(kind)


def setup_inputs(seed: int = 0) -> dict:
    keys = jax.random.split(jax.random.key(seed), 6)
    return {
        "schur_rows": draw_schur_rows(jax.random.fold_in(keys[5], 71), 0),
        "inverses": noise(keys[1], (W, NB, K), NB ** -0.5, 0.75, ((0, 16), (2, 8)), jnp.float32),
        "coupling": noise(keys[2], (W, K), 1.0, 6.0, ((0, 16),), jnp.float32),
        "selected": jax.random.permutation(keys[3], K).astype(jnp.int32),
        "schur_basis": noise(keys[4], (ROWS, W), W ** -0.5, 0.1875, ((0, 16), (1, 8))),
    }


def reference(schur_rows, inverses, coupling, selected, schur_basis):
    right_side = -jnp.take(coupling, selected, axis=1)
    solved = jnp.zeros((W, K), jnp.float32)
    for tile_index in reversed(range(W // NB)):
        row_first = tile_index * NB
        row_after = row_first + NB
        pending = right_side[row_first:row_after]
        if row_after < W:
            pending = pending - jnp.dot(schur_rows[row_first:row_after, row_after:], solved[row_after:], precision=lax.Precision.HIGHEST)
        update = jnp.sum(inverses[row_first:row_after] * pending[None, :, :], axis=1)
        solved = solved.at[row_first:row_after].set(update)
    factors = solved.astype(jnp.bfloat16)
    eigenvectors = jnp.dot(schur_basis, factors, preferred_element_type=jnp.float32).astype(jnp.bfloat16)
    return eigenvectors, solved
```

```python
import functools

import jax
import jax.numpy as jnp
from jax import lax
from jax.experimental import pallas as pl
from jax.experimental.pallas import tpu as pltpu
from jax.sharding import PartitionSpec as P

NB = 64
LANES = 128
PAIR = 2 * NB
CHIPS = 8
HIGHEST = lax.Precision.HIGHEST


SWAP = [(i, i ^ 1) for i in range(2 * CHIPS)]


def shift(values, by):
    return [(i, (i + by) % values) for i in range(values)]


def arrivals(step):
    chip = CHIPS - 1 - step
    pairs = []
    for least in (1, 2):
        chips = [(chip + k, chip - least - k) for k in range(CHIPS)]
        chips = [(a, b) for a, b in chips if a < CHIPS and b >= 0]
        pairs.append([(2 * a + core, 2 * b + core) for a, b in chips for core in (0, 1)])
    return pairs


def apply_inverse(buf, pending):
    parts = [jnp.sum(buf[pl.ds(8 * g, 8)] * pending[None], axis=1) for g in range(NB // 8)]
    return jnp.concatenate(parts, axis=0)


def step_kernel(step, *refs):
    if step:
        pend_in, x_in, xa, xb, tiles, inv, inv_other, pend_out, x_out, odd, even, sem = refs
    else:
        pend_in, tiles, inv, inv_other, pend_out, x_out, odd, even, sem = refs
    row = lax.axis_index("row")
    col = lax.axis_index("col")
    me, core = row // 2, row % 2
    chip = CHIPS - 1 - step
    active = me == chip

    def fetch(buf, which, tile):
        own = pltpu.make_async_copy(inv.at[:, :, pl.ds(pl.multiple_of(core * LANES, LANES), LANES)], buf, sem.at[which])
        other = pltpu.make_async_copy(inv_other, buf, sem.at[which])

        @pl.when(core == tile)
        def _():
            own.start()

        @pl.when(core != tile)
        def _():
            other.start()

        return own

    def product(source, x):
        slot = lax.rem(col - source + 2 * CHIPS, CHIPS)
        return jnp.dot(tiles[slot], x, precision=HIGHEST, preferred_element_type=jnp.float32)

    @pl.when(active)
    def _():
        get_odd = fetch(odd, 0, 1)
        get_even = fetch(even, 1, 0)
        if step:
            pend_out[...] = pend_in[...] - product(chip + 1, xa[...])
        else:
            pend_out[...] = pend_in[...]
        get_odd.wait()
        x_odd = apply_inverse(odd, pend_out[NB:, :])
        x_out[NB:, :] = x_odd
        slot = lax.rem(col - me + 2 * CHIPS, CHIPS)
        within = jnp.dot(tiles[slot][:NB, :], jnp.concatenate([jnp.zeros_like(x_odd), x_odd], axis=0), precision=HIGHEST, preferred_element_type=jnp.float32)
        last = pend_out[:NB, :] - within
        get_even.wait()
        x_out[:NB, :] = apply_inverse(even, last)

    @pl.when(jnp.logical_not(active))
    def _():
        pend_out[...] = pend_in[...]
        if step:
            x_out[...] = x_in[...]
            before = chip + 1
            from_a = 2 * before - 1 - me
            from_b = 2 * before - 2 - me

            @pl.when(jnp.logical_and(me < before, from_a < CHIPS))
            def _():
                pend_out[...] -= product(from_a, xa[...])

            @pl.when(jnp.logical_and(me < before - 1, from_b < CHIPS))
            def _():
                pend_out[...] -= product(from_b, xb[...])
        else:
            x_out[...] = jnp.zeros_like(x_out)


def solve_step(step, operands, inv, inv_other):
    block = jax.ShapeDtypeStruct((PAIR, LANES), jnp.float32)
    vmem = pl.BlockSpec(memory_space=pltpu.VMEM)
    hbm = pl.BlockSpec(memory_space=pl.ANY)
    return pl.pallas_call(
        functools.partial(step_kernel, step),
        out_shape=(block, block),
        in_specs=[vmem] * len(operands) + [hbm, hbm],
        out_specs=(vmem, vmem),
        scratch_shapes=[
            pltpu.VMEM((NB, NB, LANES), jnp.float32),
            pltpu.VMEM((NB, NB, LANES), jnp.float32),
            pltpu.SemaphoreType.DMA((2,)),
        ],
        compiler_params=pltpu.CompilerParams(vmem_limit_bytes=16 << 20),
        cost_estimate=pl.CostEstimate(flops=8_000_000, bytes_accessed=5_000_000, transcendentals=0),
        name="solve_step",
    )(*operands, inv, inv_other)


BLOCK = 512


def product_kernel(x_all, own, zp1, zm1, h, zp2, zm2, ra, rb, rc, rd, out):
    row = lax.axis_index("row")
    col = lax.axis_index("col")
    me = row // 2
    first = pl.program_id(0) < pl.num_programs(0) // 2

    def factor(source):
        return x_all[lax.rem(me - source + 2 * CHIPS, CHIPS)]

    def wrap(value):
        return lax.rem(value + 2 * CHIPS, CHIPS)

    partner = col + 1 - 2 * lax.rem(col, 2)

    def pair(left, right, source_left, source_right):
        lhs = jnp.concatenate([left, right], axis=1)
        rhs = jnp.concatenate([factor(source_left), factor(source_right)], axis=0)
        return jnp.dot(lhs, rhs, preferred_element_type=jnp.float32)

    far_own = jnp.where(first, ra[...], rb[...])
    far_h = jnp.where(first, rc[...], rd[...])
    total = pair(own[...], h[...], wrap(col), wrap(partner))
    total += pair(zp1[...], zp2[...], wrap(col - 2), wrap(partner - 2))
    total += pair(zm1[...], zm2[...], wrap(col + 2), wrap(partner + 2))
    total += pair(far_own, far_h, wrap(col + 4), wrap(partner + 4))
    out[...] = total.astype(out.dtype)


def back_transform(x_all, shards):
    rows = shards[0].shape[0]
    steps = rows // BLOCK
    half = steps // 2
    whole = pl.BlockSpec((BLOCK, LANES), lambda i: (i, 0))
    low = pl.BlockSpec((BLOCK, LANES), lambda i: (jnp.minimum(i, half - 1), 0))
    high = pl.BlockSpec((BLOCK, LANES), lambda i: (jnp.maximum(i - half, 0), 0))
    return pl.pallas_call(
        product_kernel,
        grid=(steps,),
        out_shape=jax.ShapeDtypeStruct((rows, 2 * LANES), jnp.bfloat16),
        in_specs=[pl.BlockSpec((CHIPS, PAIR, 2 * LANES), lambda i: (0, 0, 0))] + [whole] * 6 + [low, high, low, high],
        out_specs=pl.BlockSpec((BLOCK, 2 * LANES), lambda i: (i, 0)),
        compiler_params=pltpu.CompilerParams(vmem_limit_bytes=24 << 20),
        cost_estimate=pl.CostEstimate(flops=2 * rows * 1024 * 256, bytes_accessed=8_000_000, transcendentals=0),
        name="back_transform",
    )(x_all, *shards)


def per_device(schur_rows, inverses, coupling, selected, schur_basis):
    core = lax.axis_index("row") % 2
    is_even = core == 0

    def col_shift(value, by):
        return lax.ppermute(value, "col", shift(CHIPS, by))

    def swap(value):
        return lax.ppermute(value, "row", SWAP)

    def halves(value):
        left, right = value[..., :LANES], value[..., LANES:]
        return jnp.where(is_even, left, right), jnp.where(is_even, right, left)

    inv_other = swap(lax.dynamic_slice_in_dim(inverses, (1 - core) * LANES, LANES, 2))
    t_other = swap(schur_rows)
    t_pair = jnp.where(is_even, jnp.concatenate([schur_rows, t_other]), jnp.concatenate([t_other, schur_rows]))
    tiles = jnp.stack([t_pair] + [col_shift(t_pair, j) for j in range(1, CHIPS)])
    rhs_mine, rhs_send = halves(-jnp.take(coupling, selected, axis=1))
    rhs_other = swap(rhs_send)
    pend = jnp.where(is_even, jnp.concatenate([rhs_mine, rhs_other]), jnp.concatenate([rhs_other, rhs_mine]))

    split = schur_basis.shape[0] // 2
    zp1, zm1 = col_shift(schur_basis, 2), col_shift(schur_basis, -2)
    h = lax.ppermute(schur_basis, "col", [(i, i ^ 1) for i in range(CHIPS)])
    zp2, zm2 = col_shift(h, 2), col_shift(h, -2)
    ra, rb = col_shift(zp1[:split], 2), col_shift(zm1[split:], -2)
    rc, rd = col_shift(zp2[:split], 2), col_shift(zm2[split:], -2)

    x = None
    moved = ()
    for step in range(CHIPS):
        operands = (pend,) + ((x,) if step else ()) + moved + (tiles,)
        pend, x = solve_step(step, operands, inverses, inv_other)
        if step < CHIPS - 1:
            near, far = arrivals(step)
            moved = (
                lax.ppermute(x, "row", near),
                lax.ppermute(x, "row", far) if far else jnp.zeros_like(x),
            )

    mine = lax.dynamic_slice_in_dim(x, core * NB, NB, 0)
    theirs = swap(lax.dynamic_slice_in_dim(x, (1 - core) * NB, NB, 0))
    solved = jnp.where(is_even, jnp.concatenate([mine, theirs], axis=1), jnp.concatenate([theirs, mine], axis=1))

    factor = x.astype(jnp.bfloat16)
    parts = [factor] + [lax.ppermute(factor, "row", shift(2 * CHIPS, 2 * j)) for j in range(1, CHIPS)]
    lane = jnp.stack(parts)
    lane_other = swap(lane)
    x_all = jnp.where(is_even, jnp.concatenate([lane, lane_other], axis=2), jnp.concatenate([lane_other, lane], axis=2))
    eigen_rows = back_transform(x_all, (schur_basis, zp1, zm1, h, zp2, zm2, ra, rb, rc, rd))
    return (eigen_rows, solved)


def solution(mesh):
    in_specs = (P("row", "col"), P("row", None, "col"), P("row", None), P("col"), P("row", "col"))
    out_specs = (P("row", "col"), P("row", "col"))
    return jax.shard_map(
        per_device, mesh=mesh, in_specs=in_specs, out_specs=out_specs, check_vma=False
    )
```

```python
import functools

import jax
import jax.numpy as jnp
from jax import lax
from jax.experimental import pallas as pl
from jax.experimental.pallas import tpu as pltpu
from jax.sharding import PartitionSpec as P


NB = 64
LANES = 128
PAIR = 2 * NB
CHIPS = 8
HIGHEST = lax.Precision.HIGHEST
F32 = jnp.float32
BF16 = jnp.bfloat16


SWAP = [(i, i ^ 1) for i in range(2 * CHIPS)]
XLO = [(i, i ^ 2) for i in range(2 * CHIPS)]
XHI = [(i, i ^ 1) for i in range(CHIPS)]

VMEM = pl.BlockSpec(memory_space=pltpu.VMEM)
HBM = pl.BlockSpec(memory_space=pltpu.MemorySpace.HBM)


def shift(values, by):
    return [(i, (i + by) % values) for i in range(values)]


def moves(step):
    chip = CHIPS - 1 - step
    result = []
    for least in (1, 2, 3):
        chips = [(chip + k, chip - least - k) for k in range(CHIPS if least > 1 else 1)]
        chips = [(a, b) for a, b in chips if a < CHIPS and b >= 0]
        result.append([(2 * a + core, 2 * b + core) for a, b in chips for core in (0, 1)])
    return result


def wrap(value, size):
    return lax.rem(value + 2 * size, size)


def core_lanes(core):
    return pl.ds(pl.multiple_of(core * LANES, LANES), LANES)


def setup_kernel(coupling, selected, schur_rows, inv, inv_mine, inv_send, small, rhs_mine, sem):
    core = lax.rem(lax.axis_index("row"), 2)
    send = pltpu.make_async_copy(inv.at[:, :, core_lanes(1 - core)], inv_send, sem.at[0])
    mine = pltpu.make_async_copy(inv.at[:, :, core_lanes(core)], inv_mine, sem.at[1])
    send.start()
    mine.start()
    candidates, columns = coupling.shape[1], selected.shape[1]
    piece = 256
    total = jnp.zeros((3 * NB, columns), F32)
    for first in range(0, candidates, piece):
        part = coupling[:, first : first + piece]
        high = part.astype(BF16)
        rest = part - high.astype(F32)
        middle = rest.astype(BF16)
        low = (rest - middle.astype(F32)).astype(BF16)
        index = lax.broadcasted_iota(jnp.int32, (piece, columns), 0) + first
        chosen = jnp.where(index == selected[...], 1.0, 0.0).astype(BF16)
        total += jnp.dot(jnp.concatenate([high, middle, low], axis=0), chosen, preferred_element_type=F32)
    rhs = -(total[:NB] + total[NB : 2 * NB] + total[2 * NB :])
    left, right = rhs[:, :LANES], rhs[:, LANES:]
    rhs_mine[...] = jnp.where(core == 0, left, right)
    small[:NB, :] = schur_rows[...]
    small[NB:, :] = jnp.where(core == 0, right, left)
    send.wait()
    mine.wait()


def setup(coupling, selected, schur_rows, inverses):
    half = pltpu.VMEM((NB, NB, LANES), F32)
    return pl.pallas_call(
        setup_kernel,
        out_shape=(half, half, pltpu.VMEM((PAIR, LANES), F32), pltpu.VMEM((NB, LANES), F32)),
        in_specs=[VMEM, VMEM, VMEM, HBM],
        out_specs=(VMEM,) * 4,
        scratch_shapes=[pltpu.SemaphoreType.DMA((2,))],
        compiler_params=pltpu.CompilerParams(vmem_limit_bytes=16 << 20),
        name="setup",
    )(coupling, selected[None, :], schur_rows, pltpu.with_memory_space_constraint(inverses, pltpu.HBM))


def apply_inverse(inv, pending):
    parts = [jnp.sum(inv[pl.ds(8 * g, 8)] * pending[None], axis=1) for g in range(NB // 8)]
    return jnp.concatenate(parts, axis=0)


def step_kernel(step, names, *refs):
    ref = dict(zip(names, refs))
    if step == 0:
        get_inv = pltpu.make_async_copy(ref["inv_from"], ref["inv_other"], refs[-1])
        get_inv.start()
    row, col = lax.axis_index("row"), lax.axis_index("col")
    me, core = row // 2, lax.rem(row, 2)
    chip = CHIPS - 1 - step
    active = me == chip
    inv_mine, inv_other, pend, x = ref["inv_mine"], ref["inv_other"], ref["pend"], ref["x"]
    tiles = ref["tiles"] if step else ref["tiles_out"]

    def tile(source):
        ahead = wrap(col // 2 - source // 2, CHIPS // 2)
        across = lax.rem(col + source, 2)
        return tiles[2 * ahead + across]

    def product(source, value):
        return jnp.dot(tile(source), value, precision=HIGHEST, preferred_element_type=F32)

    if step == 0:
        for index, name in enumerate(("t0", "t1", "t2", "t3")):
            tiles[pl.ds(2 * index, 2)] = ref[name][...]
        pend[pl.ds(pl.multiple_of(core * NB, NB), NB), :] = ref["rhs_mine"][...]
        pend[pl.ds(pl.multiple_of((1 - core) * NB, NB), NB), :] = ref["small"][NB:, :]
        get_inv.wait()
    else:
        pend[...] = ref["pend_in"][...]

    @pl.when(active)
    def _():
        if step:
            total = pend[...] - product(chip + 1, ref["near"][...])
            if step > 1:
                total -= product(chip + 2, ref["far2"][...])
            pend[...] = total

        def solve(odd, even):
            x_odd = apply_inverse(odd, pend[NB:, :])
            x[NB:, :] = x_odd
            padded = jnp.concatenate([jnp.zeros_like(x_odd), x_odd], axis=0)
            within = jnp.dot(tile(me)[:NB, :], padded, precision=HIGHEST, preferred_element_type=F32)
            x[:NB, :] = apply_inverse(even, pend[:NB, :] - within)

        @pl.when(core == 1)
        def _():
            solve(inv_mine, inv_other)

        @pl.when(core == 0)
        def _():
            solve(inv_other, inv_mine)

    @pl.when(jnp.logical_not(active))
    def _():
        x[...] = ref["x_in"][...] if step else jnp.zeros_like(x)
        if step > 1:
            from2, from3 = 2 * chip + 2 - me, 2 * chip + 1 - me

            @pl.when(jnp.logical_and(me < chip, from2 < CHIPS))
            def _():
                pend[...] -= product(from2, ref["far2"][...])

            if "far3" in ref:

                @pl.when(jnp.logical_and(me < chip, from3 < CHIPS))
                def _():
                    pend[...] -= product(from3, ref["far3"][...])

    if step == CHIPS - 1:
        ref["factor"][...] = x[...].astype(BF16)
        ref["mine"][...] = x[pl.ds(pl.multiple_of(core * NB, NB), NB), :]
        ref["theirs"][...] = x[pl.ds(pl.multiple_of((1 - core) * NB, NB), NB), :]


def solve_step(step, operands):
    block = jax.ShapeDtypeStruct((PAIR, LANES), F32)
    outs = {"pend": block, "x": block}
    if step == 0:
        outs["tiles_out"] = pltpu.VMEM((CHIPS, PAIR, LANES), F32)
        outs["inv_other"] = pltpu.VMEM((NB, NB, LANES), F32)
    if step == CHIPS - 1:
        outs["factor"] = jax.ShapeDtypeStruct((PAIR, LANES), BF16)
        outs["mine"] = outs["theirs"] = jax.ShapeDtypeStruct((NB, LANES), F32)
    names = list(operands) + list(outs)
    call = pl.pallas_call(
        functools.partial(step_kernel, step, names),
        out_shape=tuple(outs.values()),
        in_specs=[HBM if name == "inv_from" else VMEM for name in operands],
        out_specs=(VMEM,) * len(outs),
        scratch_shapes=[] if step else [pltpu.SemaphoreType.DMA],
        compiler_params=pltpu.CompilerParams(vmem_limit_bytes=16 << 20),
        cost_estimate=pl.CostEstimate(flops=8_000_000, bytes_accessed=5_000_000, transcendentals=0),
        name="solve_step",
    )
    result = call(*operands.values())
    return dict(zip(outs, result))


BLOCK = 512


def stack_kernel(a, b, c, d, out):
    for index, part in enumerate((a, b, c, d)):
        out[index] = part[...]


def stack4(*parts):
    return pl.pallas_call(
        stack_kernel,
        out_shape=jax.ShapeDtypeStruct((4,) + parts[0].shape, parts[0].dtype),
        in_specs=[VMEM] * 4,
        out_specs=VMEM,
        compiler_params=pltpu.CompilerParams(vmem_limit_bytes=8 << 20),
        name="stack4",
    )(*parts)


def product_kernel(same, same_swap, cross, cross_swap, own, h, zp1, zp2, zm1, zm2, z2, z2x, out, x_all):
    row, col = lax.axis_index("row"), lax.axis_index("col")
    core, xlo, y = lax.rem(row, 2), lax.rem(row // 2, 2), row // 4

    @pl.when(pl.program_id(0) == 0)
    def _():
        for back in range(4):
            level = wrap(y - back, 4)
            x_all[2 * level + xlo, :, core_lanes(core)] = same[back]
            x_all[2 * level + xlo, :, core_lanes(1 - core)] = same_swap[back]
            x_all[2 * level + 1 - xlo, :, core_lanes(core)] = cross[back]
            x_all[2 * level + 1 - xlo, :, core_lanes(1 - core)] = cross_swap[back]

    def pair(left, right, by):
        source = wrap(col + by, CHIPS)
        other = source + 1 - 2 * lax.rem(source, 2)
        lhs = jnp.concatenate([left[...], right[...]], axis=1)
        rhs = jnp.concatenate([x_all[source], x_all[other]], axis=0)
        return jnp.dot(lhs, rhs, preferred_element_type=F32)

    total = pair(own, h, 0) + pair(zp1, zp2, -2) + pair(zm1, zm2, 2) + pair(z2, z2x, 4)
    out[...] = total.astype(out.dtype)


def back_transform(factors, shards):
    rows = shards[0].shape[0]
    block = pl.BlockSpec((BLOCK, LANES), lambda i: (i, 0))
    resident = pl.BlockSpec((4, PAIR, LANES), lambda i: (0, 0, 0))
    return pl.pallas_call(
        product_kernel,
        grid=(rows // BLOCK,),
        out_shape=jax.ShapeDtypeStruct((rows, 2 * LANES), BF16),
        in_specs=[resident] * 4 + [block] * 8,
        out_specs=pl.BlockSpec((BLOCK, 2 * LANES), lambda i: (i, 0)),
        scratch_shapes=[pltpu.VMEM((CHIPS, PAIR, 2 * LANES), BF16)],
        compiler_params=pltpu.CompilerParams(vmem_limit_bytes=16 << 20),
        cost_estimate=pl.CostEstimate(flops=2 * rows * 1024 * 256, bytes_accessed=8_000_000, transcendentals=0),
        name="back_transform",
    )(*factors, *shards)


def per_device(schur_rows, inverses, coupling, selected, schur_basis):
    is_even = lax.axis_index("row") % 2 == 0

    def col_shift(value, by):
        return lax.ppermute(value, "col", shift(CHIPS, by))

    def row_move(value, pairs):
        return lax.ppermute(value, "row", pairs)

    def across(value):
        return lax.ppermute(value, "col", XHI)

    def tile_move(value, name, moved):
        pairs = []
        for row in range(2 * CHIPS):
            for col in range(CHIPS):
                last = col if name == "tx" else col | 1
                if last >= row // 2:
                    pairs.append((row * CHIPS + col, row * CHIPS + moved(col)))
        return lax.ppermute(value, ("row", "col"), pairs)

    inv_mine, inv_send, small, rhs_mine = setup(coupling, selected, schur_rows, inverses)
    inv_other = row_move(inv_send, SWAP)
    small = row_move(small, SWAP)
    t_other = small[:NB]
    t_pair = jnp.where(is_even, jnp.concatenate([schur_rows, t_other]), jnp.concatenate([t_other, schur_rows]))
    t0 = jnp.stack([t_pair, tile_move(t_pair, "tx", lambda c: c ^ 1)])
    t1, t2, t3 = [tile_move(t0, f"tz{j}", lambda c, j=j: (c + 2 * j) % CHIPS) for j in (1, 2, 3)]

    zp1, zm1 = col_shift(schur_basis, 2), col_shift(schur_basis, -2)
    z2, h = col_shift(schur_basis, 4), across(schur_basis)

    received = {"small": small, "t0": t0, "t1": t1, "t2": t2, "t3": t3, "inv_from": inv_other}
    state = solve_step(0, {"rhs_mine": rhs_mine, "inv_mine": inv_mine, **received})
    kept = {"inv_mine": inv_mine, "inv_other": state["inv_other"], "tiles": state["tiles_out"]}
    late = {}
    for step in range(1, CHIPS):
        near, far2, far3 = moves(step - 1)
        operands = {"pend_in": state["pend"], "x_in": state["x"], "near": row_move(state["x"], near)}
        operands.update(late)
        late = {name: row_move(state["x"], pairs) for name, pairs in (("far2", far2), ("far3", far3)) if pairs}
        state = solve_step(step, {**operands, **kept})
        if step == 3:
            h, _ = lax.optimization_barrier((h, state["x"]))
            zp2, zm2 = col_shift(h, 2), col_shift(h, -2)
        if step == 4:
            z2, _ = lax.optimization_barrier((z2, state["x"]))
            z2x = across(z2)

    factor = state["factor"]
    same = stack4(factor, *[row_move(factor, shift(2 * CHIPS, 4 * j)) for j in (1, 2, 3)])
    cross = row_move(same, XLO)
    same_swap = row_move(same, SWAP)
    cross_swap = row_move(cross, SWAP)
    eigen_rows = back_transform((same, same_swap, cross, cross_swap), (schur_basis, h, zp1, zp2, zm1, zm2, z2, z2x))

    mine, theirs = state["mine"], row_move(state["theirs"], SWAP)
    solved = jnp.where(is_even, jnp.concatenate([mine, theirs], axis=1), jnp.concatenate([theirs, mine], axis=1))
    return (eigen_rows, solved)


def solution(mesh):
    in_specs = (P("row", "col"), P("row", None, "col"), P("row", None), P("col"), P("row", "col"))
    out_specs = (P("row", "col"), P("row", "col"))
    return jax.shard_map(per_device, mesh=mesh, in_specs=in_specs, out_specs=out_specs, check_vma=False)
```

```python
import functools

import jax
import jax.numpy as jnp
from jax import lax
from jax.experimental import pallas as pl
from jax.experimental.pallas import tpu as pltpu
from jax.sharding import PartitionSpec as P


NB = 64
LANES = 128
PAIR = 2 * NB
CHIPS = 8
HIGHEST = lax.Precision.HIGHEST
F32 = jnp.float32
BF16 = jnp.bfloat16


SWAP = [(i, i ^ 1) for i in range(2 * CHIPS)]
XLO = [(i, i ^ 2) for i in range(2 * CHIPS)]
XHI = [(i, i ^ 1) for i in range(CHIPS)]

VMEM = pl.BlockSpec(memory_space=pltpu.VMEM)
HBM = pl.BlockSpec(memory_space=pltpu.MemorySpace.HBM)


def shift(values, by):
    return [(i, (i + by) % values) for i in range(values)]


def moves(step):
    chip = CHIPS - 1 - step
    result = []
    for least in (1, 2, 3):
        chips = [(chip + k, chip - least - k) for k in range(CHIPS if least > 1 else 1)]
        chips = [(a, b) for a, b in chips if a < CHIPS and b >= 0]
        result.append([(2 * a + core, 2 * b + core) for a, b in chips for core in (0, 1)])
    return result


def wrap(value, size):
    return lax.rem(value + 2 * size, size)


def core_lanes(core):
    return pl.ds(pl.multiple_of(core * LANES, LANES), LANES)


def setup_kernel(coupling, selected, t0, t1, t2, t3, inv, inv_from, inv_mine, inv_other, send, rhs_mine, sem):
    core = lax.rem(lax.axis_index("row"), 2)
    mine = pltpu.make_async_copy(inv.at[:, :, core_lanes(core)], inv_mine, sem.at[0])
    other = pltpu.make_async_copy(inv_from.at[:, :, core_lanes(core)], inv_other, sem.at[1])
    mine.start()
    other.start()
    for index, tile in enumerate((t0, t1, t2, t3)):
        for half in range(2):
            send[pl.ds((2 * index + half) * NB, NB), :] = tile[half]
    candidates, columns = coupling.shape[1], selected.shape[1]
    piece = 256
    total = jnp.zeros((3 * NB, columns), F32)
    for first in range(0, candidates, piece):
        part = coupling[:, first : first + piece]
        high = part.astype(BF16)
        rest = part - high.astype(F32)
        middle = rest.astype(BF16)
        low = (rest - middle.astype(F32)).astype(BF16)
        index = lax.broadcasted_iota(jnp.int32, (piece, columns), 0) + first
        chosen = jnp.where(index == selected[...], 1.0, 0.0).astype(BF16)
        total += jnp.dot(jnp.concatenate([high, middle, low], axis=0), chosen, preferred_element_type=F32)
    rhs = -(total[:NB] + total[NB : 2 * NB] + total[2 * NB :])
    left, right = rhs[:, :LANES], rhs[:, LANES:]
    rhs_mine[...] = jnp.where(core == 0, left, right)
    send[pl.ds(CHIPS * NB, NB), :] = jnp.where(core == 0, right, left)
    mine.wait()
    other.wait()


def setup(coupling, selected, parts, inverses, inv_from):
    half = pltpu.VMEM((NB, NB, LANES), F32)
    return pl.pallas_call(
        setup_kernel,
        out_shape=(half, half, pltpu.VMEM(((CHIPS + 1) * NB, LANES), F32), pltpu.VMEM((NB, LANES), F32)),
        in_specs=[VMEM] * 6 + [HBM] * 2,
        out_specs=(VMEM,) * 4,
        scratch_shapes=[pltpu.SemaphoreType.DMA((2,))],
        compiler_params=pltpu.CompilerParams(vmem_limit_bytes=16 << 20),
        name="setup",
    )(coupling, selected[None, :], *parts, pltpu.with_memory_space_constraint(inverses, pltpu.HBM), inv_from)


def apply_inverse(inv, pending):
    parts = [jnp.sum(inv[pl.ds(8 * g, 8)] * pending[None], axis=1) for g in range(NB // 8)]
    return jnp.concatenate(parts, axis=0)


def step_kernel(step, names, *refs):
    ref = dict(zip(names, refs))
    row, col = lax.axis_index("row"), lax.axis_index("col")
    me, core = row // 2, lax.rem(row, 2)
    chip = CHIPS - 1 - step
    active = me == chip
    inv_mine, inv_other, pend, x = ref["inv_mine"], ref["inv_other"], ref["pend"], ref["x"]
    tiles = ref["tiles"] if step else ref["tiles_out"]

    def tile(source):
        ahead = wrap(col // 2 - source // 2, CHIPS // 2)
        across = lax.rem(col + source, 2)
        return tiles[2 * ahead + across]

    def product(source, value):
        return jnp.dot(tile(source), value, precision=HIGHEST, preferred_element_type=F32)

    if step == 0:
        mine = pl.ds(pl.multiple_of(core * NB, NB), NB)
        theirs = pl.ds(pl.multiple_of((1 - core) * NB, NB), NB)
        for index in range(CHIPS):
            tiles[index, mine, :] = ref["sent"][pl.ds(index * NB, NB), :]
            tiles[index, theirs, :] = ref["swapped"][pl.ds(index * NB, NB), :]
        pend[mine, :] = ref["rhs_mine"][...]
        pend[theirs, :] = ref["swapped"][pl.ds(CHIPS * NB, NB), :]
    else:
        pend[...] = ref["pend_in"][...]

    @pl.when(active)
    def _():
        if step:
            total = pend[...] - product(chip + 1, ref["near"][...])
            if step > 1:
                total -= product(chip + 2, ref["far2"][...])
            pend[...] = total

        def solve(odd, even):
            x_odd = apply_inverse(odd, pend[NB:, :])
            x[NB:, :] = x_odd
            padded = jnp.concatenate([jnp.zeros_like(x_odd), x_odd], axis=0)
            within = jnp.dot(tile(me)[:NB, :], padded, precision=HIGHEST, preferred_element_type=F32)
            x[:NB, :] = apply_inverse(even, pend[:NB, :] - within)

        @pl.when(core == 1)
        def _():
            solve(inv_mine, inv_other)

        @pl.when(core == 0)
        def _():
            solve(inv_other, inv_mine)

    @pl.when(jnp.logical_not(active))
    def _():
        x[...] = ref["x_in"][...] if step else jnp.zeros_like(x)
        if step > 1:
            from2, from3 = 2 * chip + 2 - me, 2 * chip + 1 - me

            @pl.when(jnp.logical_and(me < chip, from2 < CHIPS))
            def _():
                pend[...] -= product(from2, ref["far2"][...])

            if "far3" in ref:

                @pl.when(jnp.logical_and(me < chip, from3 < CHIPS))
                def _():
                    pend[...] -= product(from3, ref["far3"][...])

    if step == CHIPS - 1:
        ref["factor"][...] = x[...].astype(BF16)
        ref["mine"][...] = x[pl.ds(pl.multiple_of(core * NB, NB), NB), :]
        ref["theirs"][...] = x[pl.ds(pl.multiple_of((1 - core) * NB, NB), NB), :]


def solve_step(step, operands):
    block = pltpu.VMEM((PAIR, LANES), F32)
    outs = {"pend": block, "x": block}
    if step == 0:
        outs["tiles_out"] = pltpu.VMEM((CHIPS, PAIR, LANES), F32)
    if step == CHIPS - 1:
        outs["factor"] = jax.ShapeDtypeStruct((PAIR, LANES), BF16)
        outs["mine"] = outs["theirs"] = jax.ShapeDtypeStruct((NB, LANES), F32)
    names = list(operands) + list(outs)
    call = pl.pallas_call(
        functools.partial(step_kernel, step, names),
        out_shape=tuple(outs.values()),
        in_specs=[VMEM] * len(operands),
        out_specs=(VMEM,) * len(outs),
        compiler_params=pltpu.CompilerParams(vmem_limit_bytes=16 << 20),
        cost_estimate=pl.CostEstimate(flops=8_000_000, bytes_accessed=5_000_000, transcendentals=0),
        name="solve_step",
    )
    result = call(*operands.values())
    return dict(zip(outs, result))


BLOCK = 512


def stack_kernel(a, b, c, d, out):
    for index, part in enumerate((a, b, c, d)):
        out[index] = part[...]


def stack4(*parts):
    return pl.pallas_call(
        stack_kernel,
        out_shape=jax.ShapeDtypeStruct((4,) + parts[0].shape, parts[0].dtype),
        in_specs=[VMEM] * 4,
        out_specs=VMEM,
        compiler_params=pltpu.CompilerParams(vmem_limit_bytes=8 << 20),
        name="stack4",
    )(*parts)


def product_kernel(same, same_swap, cross, cross_swap, own, h, zp1, zp2, zm1, zm2, ra, rb, rc, rd, out, x_all):
    row, col = lax.axis_index("row"), lax.axis_index("col")
    core, xlo, y = lax.rem(row, 2), lax.rem(row // 2, 2), row // 4

    @pl.when(pl.program_id(0) == 0)
    def _():
        for back in range(4):
            level = wrap(y - back, 4)
            x_all[2 * level + xlo, :, core_lanes(core)] = same[back]
            x_all[2 * level + xlo, :, core_lanes(1 - core)] = same_swap[back]
            x_all[2 * level + 1 - xlo, :, core_lanes(core)] = cross[back]
            x_all[2 * level + 1 - xlo, :, core_lanes(1 - core)] = cross_swap[back]

    def pair(left, right, by):
        source = wrap(col + by, CHIPS)
        other = source + 1 - 2 * lax.rem(source, 2)
        lhs = jnp.concatenate([left, right], axis=1)
        rhs = jnp.concatenate([x_all[source], x_all[other]], axis=0)
        return jnp.dot(lhs, rhs, preferred_element_type=F32)

    first = pl.program_id(0) < pl.num_programs(0) // 2
    far_own = jnp.where(first, ra[...], rb[...])
    far_h = jnp.where(first, rc[...], rd[...])
    total = pair(own[...], h[...], 0) + pair(zp1[...], zp2[...], -2) + pair(zm1[...], zm2[...], 2)
    total += pair(far_own, far_h, 4)
    out[...] = total.astype(out.dtype)


def back_transform(factors, shards):
    rows = shards[0].shape[0]
    half = rows // BLOCK // 2
    block = pl.BlockSpec((BLOCK, LANES), lambda i: (i, 0))
    low = pl.BlockSpec((BLOCK, LANES), lambda i: (jnp.minimum(i, half - 1), 0))
    high = pl.BlockSpec((BLOCK, LANES), lambda i: (jnp.maximum(i - half, 0), 0))
    resident = pl.BlockSpec((4, PAIR, LANES), lambda i: (0, 0, 0))
    return pl.pallas_call(
        product_kernel,
        grid=(rows // BLOCK,),
        out_shape=jax.ShapeDtypeStruct((rows, 2 * LANES), BF16),
        in_specs=[resident] * 4 + [block] * 6 + [low, high, low, high],
        out_specs=pl.BlockSpec((BLOCK, 2 * LANES), lambda i: (i, 0)),
        scratch_shapes=[pltpu.VMEM((CHIPS, PAIR, 2 * LANES), BF16)],
        compiler_params=pltpu.CompilerParams(vmem_limit_bytes=16 << 20),
        cost_estimate=pl.CostEstimate(flops=2 * rows * 1024 * 256, bytes_accessed=8_000_000, transcendentals=0),
        name="back_transform",
    )(*factors, *shards)


def per_device(schur_rows, inverses, coupling, selected, schur_basis):
    is_even = lax.axis_index("row") % 2 == 0

    def col_shift(value, by):
        return lax.ppermute(value, "col", shift(CHIPS, by))

    def row_move(value, pairs):
        return lax.ppermute(value, "row", pairs)

    def across(value):
        return lax.ppermute(value, "col", XHI)

    def tile_move(value, name, moved):
        pairs = []
        for row in range(2 * CHIPS):
            for col in range(CHIPS):
                last = col if name == "tx" else col | 1
                if last >= row // 2:
                    pairs.append((row * CHIPS + col, row * CHIPS + moved(col)))
        return lax.ppermute(value, ("row", "col"), pairs)

    t0 = jnp.stack([schur_rows, tile_move(schur_rows, "tx", lambda c: c ^ 1)])
    parts = [t0] + [tile_move(t0, f"tz{j}", lambda c, j=j: (c + 2 * j) % CHIPS) for j in (1, 2, 3)]
    inv_from = row_move(inverses, SWAP)

    zp1, zm1 = col_shift(schur_basis, 2), col_shift(schur_basis, -2)
    h = across(schur_basis)
    split = schur_basis.shape[0] // 2

    inv_mine, inv_other, sent, rhs_mine = setup(coupling, selected, parts, inverses, inv_from)
    swapped = row_move(sent, SWAP)
    kept = {"inv_mine": inv_mine, "inv_other": inv_other}
    state = solve_step(0, {"rhs_mine": rhs_mine, "sent": sent, "swapped": swapped, **kept})
    kept["tiles"] = state["tiles_out"]
    late = {}
    for step in range(1, CHIPS):
        near, far2, far3 = moves(step - 1)
        operands = {"pend_in": state["pend"], "x_in": state["x"], "near": row_move(state["x"], near)}
        operands.update(late)
        late = {name: row_move(state["x"], pairs) for name, pairs in (("far2", far2), ("far3", far3)) if pairs}
        state = solve_step(step, {**operands, **kept})
        if step == 2:
            h, _ = lax.optimization_barrier((h, state["x"]))
            zp2, zm2 = col_shift(h, 2), col_shift(h, -2)
        if step == 3:
            zp1, zm1, _ = lax.optimization_barrier((zp1, zm1, state["x"]))
            ra, rb = col_shift(zp1[:split], 2), col_shift(zm1[split:], -2)
        if step == 6:
            zp2, zm2, _ = lax.optimization_barrier((zp2, zm2, state["x"]))
            rc, rd = col_shift(zp2[:split], 2), col_shift(zm2[split:], -2)

    factor = state["factor"]
    same = stack4(factor, *[row_move(factor, shift(2 * CHIPS, 4 * j)) for j in (1, 2, 3)])
    cross = row_move(same, XLO)
    same_swap = row_move(same, SWAP)
    cross_swap = row_move(cross, SWAP)
    eigen_rows = back_transform((same, same_swap, cross, cross_swap), (schur_basis, h, zp1, zp2, zm1, zm2, ra, rb, rc, rd))

    mine, theirs = state["mine"], row_move(state["theirs"], SWAP)
    solved = jnp.where(is_even, jnp.concatenate([mine, theirs], axis=1), jnp.concatenate([theirs, mine], axis=1))
    return (eigen_rows, solved)


def solution(mesh):
    in_specs = (P("row", "col"), P("row", None, "col"), P("row", None), P("col"), P("row", "col"))
    out_specs = (P("row", "col"), P("row", "col"))
    return jax.shard_map(per_device, mesh=mesh, in_specs=in_specs, out_specs=out_specs, check_vma=False)
```

```python
import functools

import jax
import jax.numpy as jnp
from jax import lax
from jax.experimental import pallas as pl
from jax.experimental.pallas import tpu as pltpu
from jax.sharding import PartitionSpec as P


NB = 64
LANES = 128
PAIR = 2 * NB
CHIPS = 8
HIGHEST = lax.Precision.HIGHEST
F32 = jnp.float32
BF16 = jnp.bfloat16


VMEM = pl.BlockSpec(memory_space=pltpu.VMEM)
HBM = pl.BlockSpec(memory_space=pltpu.MemorySpace.HBM)


def flip(values, mask):
    return [(i, i ^ mask) for i in range(values)]


def moves(step):
    chip = CHIPS - 1 - step
    result = []
    for least in (1, 2, 3):
        chips = [(chip + k, chip - least - k) for k in range(CHIPS if least > 1 else 1)]
        chips = [(a, b) for a, b in chips if a < CHIPS and b >= 0]
        result.append([(2 * a + core, 2 * b + core) for a, b in chips for core in (0, 1)])
    return result


def core_lanes(core):
    return pl.ds(pl.multiple_of(core * LANES, LANES), LANES)


def setup_kernel(candidates_from, selected_from, t0, t1, t2, t3, inv, inv_from, inv_mine, inv_other, send, rhs_mine, coupling, selected, sem):
    core = lax.rem(lax.axis_index("row"), 2)
    copies = [
        pltpu.make_async_copy(candidates_from, coupling, sem.at[0]),
        pltpu.make_async_copy(selected_from, selected, sem.at[1]),
        pltpu.make_async_copy(inv.at[:, :, core_lanes(core)], inv_mine, sem.at[2]),
        pltpu.make_async_copy(inv_from.at[:, :, core_lanes(core)], inv_other, sem.at[3]),
    ]
    for copy in copies:
        copy.start()
    for index, tile in enumerate((t0, t1, t2, t3)):
        for half in range(2):
            send[pl.ds((2 * index + half) * NB, NB), :] = tile[half]
    copies[0].wait()
    copies[1].wait()
    candidates, columns = coupling.shape[1], selected.shape[1]
    piece = 256
    total = jnp.zeros((3 * NB, columns), F32)
    for first in range(0, candidates, piece):
        part = coupling[:, first : first + piece]
        high = part.astype(BF16)
        rest = part - high.astype(F32)
        middle = rest.astype(BF16)
        low = (rest - middle.astype(F32)).astype(BF16)
        index = lax.broadcasted_iota(jnp.int32, (piece, columns), 0) + first
        chosen = jnp.where(index == selected[...], 1.0, 0.0).astype(BF16)
        total += jnp.dot(jnp.concatenate([high, middle, low], axis=0), chosen, preferred_element_type=F32)
    rhs = -(total[:NB] + total[NB : 2 * NB] + total[2 * NB :])
    left, right = rhs[:, :LANES], rhs[:, LANES:]
    rhs_mine[...] = jnp.where(core == 0, left, right)
    send[pl.ds(CHIPS * NB, NB), :] = jnp.where(core == 0, right, left)
    copies[2].wait()
    copies[3].wait()


def setup(coupling, selected, parts, inverses, inv_from):
    half = pltpu.VMEM((NB, NB, LANES), F32)
    return pl.pallas_call(
        setup_kernel,
        out_shape=(half, half, pltpu.VMEM(((CHIPS + 1) * NB, LANES), F32), pltpu.VMEM((NB, LANES), F32)),
        in_specs=[HBM] * 2 + [VMEM] * 4 + [HBM] * 2,
        out_specs=(VMEM,) * 4,
        scratch_shapes=[
            pltpu.VMEM(coupling.shape, F32),
            pltpu.VMEM((1, selected.shape[0]), jnp.int32),
            pltpu.SemaphoreType.DMA((4,)),
        ],
        compiler_params=pltpu.CompilerParams(vmem_limit_bytes=16 << 20),
        name="setup",
    )(hbm(coupling), hbm(selected[None, :]), *parts, hbm(inverses), inv_from)


def hbm(value):
    return pltpu.with_memory_space_constraint(value, pltpu.HBM)


def apply_inverse(inv, pending):
    parts = [jnp.sum(inv[pl.ds(8 * g, 8)] * pending[None], axis=1) for g in range(NB // 8)]
    return jnp.concatenate(parts, axis=0)


def step_kernel(step, names, *refs):
    ref = dict(zip(names, refs))
    row, col = lax.axis_index("row"), lax.axis_index("col")
    me, core = row // 2, lax.rem(row, 2)
    chip = CHIPS - 1 - step
    active = me == chip
    inv_mine, inv_other, pend, x = ref["inv_mine"], ref["inv_other"], ref["pend"], ref["x"]
    tiles = ref["tiles"] if step else ref["tiles_out"]

    def tile(source):
        return tiles[lax.bitwise_xor(col, source)]

    def product(source, value):
        return jnp.dot(tile(source), value, precision=HIGHEST, preferred_element_type=F32)

    if step == 0:
        mine = pl.ds(pl.multiple_of(core * NB, NB), NB)
        theirs = pl.ds(pl.multiple_of((1 - core) * NB, NB), NB)
        for index in range(CHIPS):
            tiles[index, mine, :] = ref["sent"][pl.ds(index * NB, NB), :]
            tiles[index, theirs, :] = ref["swapped"][pl.ds(index * NB, NB), :]
        pend[mine, :] = ref["rhs_mine"][...]
        pend[theirs, :] = ref["swapped"][pl.ds(CHIPS * NB, NB), :]
    else:
        pend[...] = ref["pend_in"][...]

    @pl.when(active)
    def _():
        if step:
            total = pend[...] - product(chip + 1, ref["near"][...])
            if step > 1:
                total -= product(chip + 2, ref["far2"][...])
            pend[...] = total

        def solve(odd, even):
            x_odd = apply_inverse(odd, pend[NB:, :])
            x[NB:, :] = x_odd
            padded = jnp.concatenate([jnp.zeros_like(x_odd), x_odd], axis=0)
            within = jnp.dot(tile(me)[:NB, :], padded, precision=HIGHEST, preferred_element_type=F32)
            x[:NB, :] = apply_inverse(even, pend[:NB, :] - within)

        @pl.when(core == 1)
        def _():
            solve(inv_mine, inv_other)

        @pl.when(core == 0)
        def _():
            solve(inv_other, inv_mine)

    @pl.when(jnp.logical_not(active))
    def _():
        x[...] = ref["x_in"][...] if step else jnp.zeros_like(x)
        if step > 1:
            from2, from3 = 2 * chip + 2 - me, 2 * chip + 1 - me

            @pl.when(jnp.logical_and(me < chip, from2 < CHIPS))
            def _():
                pend[...] -= product(from2, ref["far2"][...])

            if "far3" in ref:

                @pl.when(jnp.logical_and(me < chip, from3 < CHIPS))
                def _():
                    pend[...] -= product(from3, ref["far3"][...])

    if step == CHIPS - 1:
        ref["factor"][...] = x[...].astype(BF16)
        ref["mine"][...] = x[pl.ds(pl.multiple_of(core * NB, NB), NB), :]
        ref["theirs"][...] = x[pl.ds(pl.multiple_of((1 - core) * NB, NB), NB), :]


def solve_step(step, operands):
    block = pltpu.VMEM((PAIR, LANES), F32)
    outs = {"pend": block, "x": block}
    if step == 0:
        outs["tiles_out"] = pltpu.VMEM((CHIPS, PAIR, LANES), F32)
    if step == CHIPS - 1:
        outs["factor"] = pltpu.VMEM((PAIR, LANES), BF16)
        outs["mine"] = outs["theirs"] = pltpu.VMEM((NB, LANES), F32)
    names = list(operands) + list(outs)
    call = pl.pallas_call(
        functools.partial(step_kernel, step, names),
        out_shape=tuple(outs.values()),
        in_specs=[VMEM] * len(operands),
        out_specs=(VMEM,) * len(outs),
        compiler_params=pltpu.CompilerParams(vmem_limit_bytes=16 << 20),
        cost_estimate=pl.CostEstimate(flops=8_000_000, bytes_accessed=5_000_000, transcendentals=0),
        name="solve_step",
    )
    result = call(*operands.values())
    return dict(zip(outs, result))


BLOCK = 512


def stack_kernel(a, b, c, d, out):
    for index, part in enumerate((a, b, c, d)):
        out[index] = part[...]


def stack4(*parts):
    return pl.pallas_call(
        stack_kernel,
        out_shape=jax.ShapeDtypeStruct((4,) + parts[0].shape, parts[0].dtype),
        in_specs=[VMEM] * 4,
        out_specs=VMEM,
        compiler_params=pltpu.CompilerParams(vmem_limit_bytes=8 << 20),
        name="stack4",
    )(*parts)


def product_kernel(same, same_swap, cross, cross_swap, mine, theirs, v0, v1, v2, v3, a4, b4, a5, b5, v6, v7, out, slab, x_all):
    row, col = lax.axis_index("row"), lax.axis_index("col")
    core, xlo, y = lax.rem(row, 2), lax.rem(row // 2, 2), row // 4

    @pl.when(pl.program_id(0) == 0)
    def _():
        for mask in range(4):
            source = 2 * lax.bitwise_xor(y, mask) + xlo
            for index, left, right in ((source, same, same_swap), (lax.bitwise_xor(source, 1), cross, cross_swap)):
                slot = pl.ds(pl.multiple_of(lax.bitwise_xor(col, index) * PAIR, PAIR), PAIR)
                x_all[slot, core_lanes(core)] = left[mask]
                x_all[slot, core_lanes(1 - core)] = right[mask]
        slab[:, core_lanes(core)] = mine[...]
        slab[:, core_lanes(1 - core)] = theirs[...]

    first = pl.program_id(0) < pl.num_programs(0) // 2
    half = pl.num_programs(0) // 2
    rows = pl.ds(pl.multiple_of(pl.program_id(0) * BLOCK, BLOCK), BLOCK)
    part = pl.ds(pl.multiple_of(lax.rem(pl.program_id(0), half) * BLOCK, BLOCK), BLOCK)
    v4 = jnp.where(first, a4[part, :], b4[part, :])
    v5 = jnp.where(first, a5[part, :], b5[part, :])
    lhs = jnp.concatenate([v0[rows, :], v1[rows, :], v2[rows, :], v3[rows, :], v4, v5, v6[rows, :], v7[rows, :]], axis=1)
    out[...] = jnp.dot(lhs, x_all[...], preferred_element_type=F32).astype(out.dtype)


def back_transform(factors, slabs, shards):
    rows = shards[0].shape[0]
    half = rows // BLOCK // 2
    block = pl.BlockSpec((BLOCK, LANES), lambda i: (i, 0))
    low = pl.BlockSpec((BLOCK, LANES), lambda i: (jnp.minimum(i, half - 1), 0))
    high = pl.BlockSpec((BLOCK, LANES), lambda i: (jnp.maximum(i - half, 0), 0))
    return pl.pallas_call(
        product_kernel,
        grid=(rows // BLOCK,),
        out_shape=(
            jax.ShapeDtypeStruct((rows, 2 * LANES), BF16),
            jax.ShapeDtypeStruct((NB, 2 * LANES), F32),
        ),
        in_specs=[VMEM] * 16,
        out_specs=(pl.BlockSpec((BLOCK, 2 * LANES), lambda i: (i, 0)), VMEM),
        scratch_shapes=[pltpu.VMEM((CHIPS * PAIR, 2 * LANES), BF16)],
        compiler_params=pltpu.CompilerParams(vmem_limit_bytes=24 << 20),
        cost_estimate=pl.CostEstimate(flops=2 * rows * 1024 * 256, bytes_accessed=8_000_000, transcendentals=0),
        name="back_transform",
    )(*factors, *slabs, *shards)


def per_device(schur_rows, inverses, coupling, selected, schur_basis):
    def col_flip(value, mask):
        return lax.ppermute(value, "col", flip(CHIPS, mask))

    def row_move(value, pairs):
        return lax.ppermute(value, "row", pairs)

    def row_flip(value, mask):
        return row_move(value, flip(2 * CHIPS, mask))

    t0 = jnp.stack([schur_rows, col_flip(schur_rows, 1)])
    parts = [t0] + [col_flip(t0, mask) for mask in (2, 4, 6)]
    inv_from = row_flip(inverses, 1)

    v = {0: schur_basis, 1: col_flip(schur_basis, 1)}
    v[2], v[6] = col_flip(schur_basis, 2), col_flip(schur_basis, 6)
    split = schur_basis.shape[0] // 2

    inv_mine, inv_other, sent, rhs_mine = setup(coupling, selected, parts, inverses, inv_from)
    swapped = row_flip(sent, 1)
    kept = {"inv_mine": inv_mine, "inv_other": inv_other}
    state = solve_step(0, {"rhs_mine": rhs_mine, "sent": sent, "swapped": swapped, **kept})
    kept["tiles"] = state["tiles_out"]
    late = {}
    for step in range(1, CHIPS):
        near, far2, far3 = moves(step - 1)
        operands = {"pend_in": state["pend"], "x_in": state["x"], "near": row_move(state["x"], near)}
        operands.update(late)
        late = {name: row_move(state["x"], pairs) for name, pairs in (("far2", far2), ("far3", far3)) if pairs}
        state = solve_step(step, {**operands, **kept})
        if step == 2:
            v[1], _ = lax.optimization_barrier((v[1], state["x"]))
            v[3], v[7] = col_flip(v[1], 2), col_flip(v[1], 6)
        if step == 3:
            v[2], v[6], _ = lax.optimization_barrier((v[2], v[6], state["x"]))
            a4, b4 = col_flip(v[6][:split], 2), col_flip(v[2][split:], 6)
        if step == 6:
            v[3], v[7], _ = lax.optimization_barrier((v[3], v[7], state["x"]))
            a5, b5 = col_flip(v[7][:split], 2), col_flip(v[3][split:], 6)

    factor = state["factor"]
    same = stack4(factor, *[row_flip(factor, 4 * mask) for mask in (1, 2, 3)])
    cross = row_flip(same, 2)
    factors = (same, row_flip(same, 1), cross, row_flip(cross, 1))
    slabs = (state["mine"], row_flip(state["theirs"], 1))
    return back_transform(factors, slabs, (v[0], v[1], v[2], v[3], a4, b4, a5, b5, v[6], v[7]))


def solution(mesh):
    in_specs = (P("row", "col"), P("row", None, "col"), P("row", None), P("col"), P("row", "col"))
    out_specs = (P("row", "col"), P("row", "col"))
    return jax.shard_map(per_device, mesh=mesh, in_specs=in_specs, out_specs=out_specs, check_vma=False)
```

```python
import functools

import jax
import jax.numpy as jnp
from jax import lax
from jax.experimental import pallas as pl
from jax.experimental.pallas import tpu as pltpu
from jax.sharding import PartitionSpec as P


NB = 64
LANES = 128
PAIR = 2 * NB
CHIPS = 8
HIGHEST = lax.Precision.HIGHEST
F32 = jnp.float32
BF16 = jnp.bfloat16


VMEM = pl.BlockSpec(memory_space=pltpu.VMEM)
HBM = pl.BlockSpec(memory_space=pltpu.MemorySpace.HBM)


def flip(values, mask):
    return [(i, i ^ mask) for i in range(values)]


def moves(step):
    chip = CHIPS - 1 - step
    result = []
    for least in (1, 2, 3):
        chips = [(chip + k, chip - least - k) for k in range(CHIPS if least > 1 else 1)]
        chips = [(a, b) for a, b in chips if a < CHIPS and b >= 0]
        result.append([(2 * a + core, 2 * b + core) for a, b in chips for core in (0, 1)])
    return result


def core_lanes(core):
    return pl.ds(pl.multiple_of(core * LANES, LANES), LANES)


def setup_kernel(candidates_from, selected_from, inv, inv_from, inv_mine, inv_other, rhs_mine, rhs_send, coupling, selected, sem):
    core = lax.rem(lax.axis_index("row"), 2)
    copies = [
        pltpu.make_async_copy(candidates_from, coupling, sem.at[0]),
        pltpu.make_async_copy(selected_from, selected, sem.at[1]),
        pltpu.make_async_copy(inv.at[:, :, core_lanes(core)], inv_mine, sem.at[2]),
        pltpu.make_async_copy(inv_from.at[:, :, core_lanes(core)], inv_other, sem.at[3]),
    ]
    for copy in copies:
        copy.start()
    copies[0].wait()
    copies[1].wait()
    candidates, columns = coupling.shape[1], selected.shape[1]
    piece = 256
    total = jnp.zeros((3 * NB, columns), F32)
    for first in range(0, candidates, piece):
        part = coupling[:, first : first + piece]
        high = part.astype(BF16)
        rest = part - high.astype(F32)
        middle = rest.astype(BF16)
        low = (rest - middle.astype(F32)).astype(BF16)
        index = lax.broadcasted_iota(jnp.int32, (piece, columns), 0) + first
        chosen = jnp.where(index == selected[...], 1.0, 0.0).astype(BF16)
        total += jnp.dot(jnp.concatenate([high, middle, low], axis=0), chosen, preferred_element_type=F32)
    rhs = -(total[:NB] + total[NB : 2 * NB] + total[2 * NB :])
    left, right = rhs[:, :LANES], rhs[:, LANES:]
    rhs_mine[...] = jnp.where(core == 0, left, right)
    rhs_send[...] = jnp.where(core == 0, right, left)
    copies[2].wait()
    copies[3].wait()


def setup(coupling, selected, inverses, inv_from):
    half = pltpu.VMEM((NB, NB, LANES), F32)
    side = pltpu.VMEM((NB, LANES), F32)
    return pl.pallas_call(
        setup_kernel,
        out_shape=(half, half, side, side),
        in_specs=[HBM] * 4,
        out_specs=(VMEM,) * 4,
        scratch_shapes=[
            pltpu.VMEM(coupling.shape, F32),
            pltpu.VMEM((1, selected.shape[0]), jnp.int32),
            pltpu.SemaphoreType.DMA((4,)),
        ],
        compiler_params=pltpu.CompilerParams(vmem_limit_bytes=16 << 20),
        cost_estimate=pl.CostEstimate(flops=100_000_000, bytes_accessed=5_000_000, transcendentals=0),
        name="setup",
    )(hbm(coupling), hbm(selected[None, :]), hbm(inverses), inv_from)


def join_kernel(t0, t1, t2, t3, rhs_send, send):
    for index, tile in enumerate((t0, t1, t2, t3)):
        for half in range(2):
            send[pl.ds((2 * index + half) * NB, NB), :] = tile[half]
    send[pl.ds(CHIPS * NB, NB), :] = rhs_send[...]


def join(parts, rhs_send):
    return pl.pallas_call(
        join_kernel,
        out_shape=pltpu.VMEM(((CHIPS + 1) * NB, LANES), F32),
        in_specs=[VMEM] * 5,
        out_specs=VMEM,
        compiler_params=pltpu.CompilerParams(vmem_limit_bytes=8 << 20),
        name="join",
    )(*parts, rhs_send)


def hbm(value):
    return pltpu.with_memory_space_constraint(value, pltpu.HBM)


def apply_inverse(inv, pending):
    parts = [jnp.sum(inv[pl.ds(8 * g, 8)] * pending[None], axis=1) for g in range(NB // 8)]
    return jnp.concatenate(parts, axis=0)


def step_kernel(step, names, *refs):
    ref = dict(zip(names, refs))
    row, col = lax.axis_index("row"), lax.axis_index("col")
    me, core = row // 2, lax.rem(row, 2)
    chip = CHIPS - 1 - step
    active = me == chip
    inv_mine, inv_other, pend, x = ref["inv_mine"], ref["inv_other"], ref["pend"], ref["x"]
    tiles = ref["tiles"] if step else ref["tiles_out"]

    def tile(source):
        return tiles[lax.bitwise_xor(col, source)]

    def product(source, value):
        return jnp.dot(tile(source), value, precision=HIGHEST, preferred_element_type=F32)

    if step == 0:
        mine = pl.ds(pl.multiple_of(core * NB, NB), NB)
        theirs = pl.ds(pl.multiple_of((1 - core) * NB, NB), NB)
        for index in range(CHIPS):
            tiles[index, mine, :] = ref["sent"][pl.ds(index * NB, NB), :]
            tiles[index, theirs, :] = ref["swapped"][pl.ds(index * NB, NB), :]
        pend[mine, :] = ref["rhs_mine"][...]
        pend[theirs, :] = ref["swapped"][pl.ds(CHIPS * NB, NB), :]
    else:
        pend[...] = ref["pend_in"][...]

    @pl.when(active)
    def _():
        if step:
            total = pend[...] - product(chip + 1, ref["near"][...])
            if step > 1:
                total -= product(chip + 2, ref["far2"][...])
            pend[...] = total

        def solve(odd, even):
            x_odd = apply_inverse(odd, pend[NB:, :])
            x[NB:, :] = x_odd
            padded = jnp.concatenate([jnp.zeros_like(x_odd), x_odd], axis=0)
            within = jnp.dot(tile(me)[:NB, :], padded, precision=HIGHEST, preferred_element_type=F32)
            x[:NB, :] = apply_inverse(even, pend[:NB, :] - within)

        @pl.when(core == 1)
        def _():
            solve(inv_mine, inv_other)

        @pl.when(core == 0)
        def _():
            solve(inv_other, inv_mine)

    @pl.when(jnp.logical_not(active))
    def _():
        x[...] = ref["x_in"][...] if step else jnp.zeros_like(x)
        if step > 1:
            from2, from3 = 2 * chip + 2 - me, 2 * chip + 1 - me

            @pl.when(jnp.logical_and(me < chip, from2 < CHIPS))
            def _():
                pend[...] -= product(from2, ref["far2"][...])

            if "far3" in ref:

                @pl.when(jnp.logical_and(me < chip, from3 < CHIPS))
                def _():
                    pend[...] -= product(from3, ref["far3"][...])

    if step == CHIPS - 1:
        ref["factor"][...] = x[...].astype(BF16)
        ref["mine"][...] = x[pl.ds(pl.multiple_of(core * NB, NB), NB), :]
        ref["theirs"][...] = x[pl.ds(pl.multiple_of((1 - core) * NB, NB), NB), :]


def solve_step(step, operands):
    block = pltpu.VMEM((PAIR, LANES), F32)
    outs = {"pend": block, "x": block}
    if step == 0:
        outs["tiles_out"] = pltpu.VMEM((CHIPS, PAIR, LANES), F32)
    if step == CHIPS - 1:
        outs["factor"] = pltpu.VMEM((PAIR, LANES), BF16)
        outs["mine"] = outs["theirs"] = pltpu.VMEM((NB, LANES), F32)
    names = list(operands) + list(outs)
    call = pl.pallas_call(
        functools.partial(step_kernel, step, names),
        out_shape=tuple(outs.values()),
        in_specs=[VMEM] * len(operands),
        out_specs=(VMEM,) * len(outs),
        compiler_params=pltpu.CompilerParams(vmem_limit_bytes=16 << 20),
        cost_estimate=pl.CostEstimate(flops=8_000_000, bytes_accessed=5_000_000, transcendentals=0),
        name="solve_step",
    )
    result = call(*operands.values())
    return dict(zip(outs, result))


BLOCK = 512


def stack_kernel(a, b, c, d, out):
    for index, part in enumerate((a, b, c, d)):
        out[index] = part[...]


def stack4(*parts):
    return pl.pallas_call(
        stack_kernel,
        out_shape=jax.ShapeDtypeStruct((4,) + parts[0].shape, parts[0].dtype),
        in_specs=[VMEM] * 4,
        out_specs=VMEM,
        compiler_params=pltpu.CompilerParams(vmem_limit_bytes=8 << 20),
        name="stack4",
    )(*parts)


def product_kernel(same, same_swap, cross, cross_swap, mine, theirs, v0, v1, v2, v3, a4, b4, a5, b5, v6, v7, out, slab, x_all):
    row, col = lax.axis_index("row"), lax.axis_index("col")
    core, xlo, y = lax.rem(row, 2), lax.rem(row // 2, 2), row // 4

    @pl.when(pl.program_id(0) == 0)
    def _():
        for mask in range(4):
            source = 2 * lax.bitwise_xor(y, mask) + xlo
            for index, left, right in ((source, same, same_swap), (lax.bitwise_xor(source, 1), cross, cross_swap)):
                slot = pl.ds(pl.multiple_of(lax.bitwise_xor(col, index) * PAIR, PAIR), PAIR)
                x_all[slot, core_lanes(core)] = left[mask]
                x_all[slot, core_lanes(1 - core)] = right[mask]
        slab[:, core_lanes(core)] = mine[...]
        slab[:, core_lanes(1 - core)] = theirs[...]

    first = pl.program_id(0) < pl.num_programs(0) // 2
    half = pl.num_programs(0) // 2
    rows = pl.ds(pl.multiple_of(pl.program_id(0) * BLOCK, BLOCK), BLOCK)
    part = pl.ds(pl.multiple_of(lax.rem(pl.program_id(0), half) * BLOCK, BLOCK), BLOCK)
    v4 = jnp.where(first, a4[part, :], b4[part, :])
    v5 = jnp.where(first, a5[part, :], b5[part, :])
    lhs = jnp.concatenate([v0[rows, :], v1[rows, :], v2[rows, :], v3[rows, :], v4, v5, v6[rows, :], v7[rows, :]], axis=1)
    out[...] = jnp.dot(lhs, x_all[...], preferred_element_type=F32).astype(out.dtype)


def back_transform(factors, slabs, shards):
    rows = shards[0].shape[0]
    half = rows // BLOCK // 2
    block = pl.BlockSpec((BLOCK, LANES), lambda i: (i, 0))
    low = pl.BlockSpec((BLOCK, LANES), lambda i: (jnp.minimum(i, half - 1), 0))
    high = pl.BlockSpec((BLOCK, LANES), lambda i: (jnp.maximum(i - half, 0), 0))
    return pl.pallas_call(
        product_kernel,
        grid=(rows // BLOCK,),
        out_shape=(
            jax.ShapeDtypeStruct((rows, 2 * LANES), BF16),
            jax.ShapeDtypeStruct((NB, 2 * LANES), F32),
        ),
        in_specs=[VMEM] * 16,
        out_specs=(pl.BlockSpec((BLOCK, 2 * LANES), lambda i: (i, 0)), VMEM),
        scratch_shapes=[pltpu.VMEM((CHIPS * PAIR, 2 * LANES), BF16)],
        compiler_params=pltpu.CompilerParams(vmem_limit_bytes=24 << 20),
        cost_estimate=pl.CostEstimate(flops=2 * rows * 1024 * 256, bytes_accessed=8_000_000, transcendentals=0),
        name="back_transform",
    )(*factors, *slabs, *shards)


def per_device(schur_rows, inverses, coupling, selected, schur_basis):
    def col_flip(value, mask):
        return lax.ppermute(value, "col", flip(CHIPS, mask))

    def row_move(value, pairs):
        return lax.ppermute(value, "row", pairs)

    def row_flip(value, mask):
        return row_move(value, flip(2 * CHIPS, mask))

    t0 = jnp.stack([schur_rows, col_flip(schur_rows, 1)])
    parts = [t0] + [col_flip(t0, mask) for mask in (2, 4, 6)]
    inv_from = row_flip(inverses, 1)

    v = {0: schur_basis, 1: col_flip(schur_basis, 1)}
    v[2], v[6] = col_flip(schur_basis, 2), col_flip(schur_basis, 6)
    split = schur_basis.shape[0] // 2

    inv_mine, inv_other, rhs_mine, rhs_send = setup(coupling, selected, inverses, inv_from)
    sent = join(parts, rhs_send)
    swapped = row_flip(sent, 1)
    kept = {"inv_mine": inv_mine, "inv_other": inv_other}
    state = solve_step(0, {"rhs_mine": rhs_mine, "sent": sent, "swapped": swapped, **kept})
    kept["tiles"] = state["tiles_out"]
    late = {}
    for step in range(1, CHIPS):
        near, far2, far3 = moves(step - 1)
        operands = {"pend_in": state["pend"], "x_in": state["x"], "near": row_move(state["x"], near)}
        operands.update(late)
        late = {name: row_move(state["x"], pairs) for name, pairs in (("far2", far2), ("far3", far3)) if pairs}
        state = solve_step(step, {**operands, **kept})
        if step == 2:
            v[1], _ = lax.optimization_barrier((v[1], state["x"]))
            v[3], v[7] = col_flip(v[1], 2), col_flip(v[1], 6)
        if step == 3:
            v[2], v[6], _ = lax.optimization_barrier((v[2], v[6], state["x"]))
            a4, b4 = col_flip(v[6][:split], 2), col_flip(v[2][split:], 6)
        if step == 6:
            v[3], v[7], _ = lax.optimization_barrier((v[3], v[7], state["x"]))
            a5, b5 = col_flip(v[7][:split], 2), col_flip(v[3][split:], 6)

    factor = state["factor"]
    same = stack4(factor, *[row_flip(factor, 4 * mask) for mask in (1, 2, 3)])
    cross = row_flip(same, 2)
    factors = (same, row_flip(same, 1), cross, row_flip(cross, 1))
    slabs = (state["mine"], row_flip(state["theirs"], 1))
    return back_transform(factors, slabs, (v[0], v[1], v[2], v[3], a4, b4, a5, b5, v[6], v[7]))


def solution(mesh):
    in_specs = (P("row", "col"), P("row", None, "col"), P("row", None), P("col"), P("row", "col"))
    out_specs = (P("row", "col"), P("row", "col"))
    return jax.shard_map(per_device, mesh=mesh, in_specs=in_specs, out_specs=out_specs, check_vma=False)
```

```python
import functools

import jax
import jax.numpy as jnp
from jax import lax
from jax.experimental import pallas as pl
from jax.experimental.pallas import tpu as pltpu
from jax.sharding import PartitionSpec as P


NB = 64
LANES = 128
PAIR = 2 * NB
CHIPS = 8
F32 = jnp.float32
BF16 = jnp.bfloat16


VMEM = pl.BlockSpec(memory_space=pltpu.VMEM)
HBM = pl.BlockSpec(memory_space=pltpu.MemorySpace.HBM)


def flip(values, mask):
    return [(i, i ^ mask) for i in range(values)]


def moves(step):
    chip = CHIPS - 1 - step
    result = []
    for least in (1, 2, 3):
        chips = [(chip + k, chip - least - k) for k in range(CHIPS if least > 1 else 1)]
        chips = [(a, b) for a, b in chips if a < CHIPS and b >= 0]
        result.append([(2 * a + core, 2 * b + core) for a, b in chips for core in (0, 1)])
    return result


def core_lanes(core):
    return pl.ds(pl.multiple_of(core * LANES, LANES), LANES)


def setup_kernel(candidates_from, selected_from, inv, inv_from, inv_mine, inv_other, rhs_mine, rhs_send, coupling, selected, sem):
    core = lax.rem(lax.axis_index("row"), 2)
    copies = [
        pltpu.make_async_copy(candidates_from, coupling, sem.at[0]),
        pltpu.make_async_copy(selected_from, selected, sem.at[1]),
        pltpu.make_async_copy(inv.at[:, :, core_lanes(core)], inv_mine, sem.at[2]),
        pltpu.make_async_copy(inv_from.at[:, :, core_lanes(core)], inv_other, sem.at[3]),
    ]
    for copy in copies:
        copy.start()
    copies[0].wait()
    copies[1].wait()
    candidates, columns = coupling.shape[1], selected.shape[1]
    piece = 256
    total = jnp.zeros((3 * NB, columns), F32)
    for first in range(0, candidates, piece):
        part = coupling[:, first : first + piece]
        high = part.astype(BF16)
        rest = part - high.astype(F32)
        middle = rest.astype(BF16)
        low = (rest - middle.astype(F32)).astype(BF16)
        index = lax.broadcasted_iota(jnp.int32, (piece, columns), 0) + first
        chosen = jnp.where(index == selected[...], 1.0, 0.0).astype(BF16)
        total += jnp.dot(jnp.concatenate([high, middle, low], axis=0), chosen, preferred_element_type=F32)
    rhs = -(total[:NB] + total[NB : 2 * NB] + total[2 * NB :])
    left, right = rhs[:, :LANES], rhs[:, LANES:]
    rhs_mine[...] = jnp.where(core == 0, left, right)
    rhs_send[...] = jnp.where(core == 0, right, left)
    copies[2].wait()
    copies[3].wait()


def setup(coupling, selected, inverses, inv_from):
    half = pltpu.VMEM((NB, NB, LANES), F32)
    side = pltpu.VMEM((NB, LANES), F32)
    return pl.pallas_call(
        setup_kernel,
        out_shape=(half, half, side, side),
        in_specs=[HBM] * 4,
        out_specs=(VMEM,) * 4,
        scratch_shapes=[
            pltpu.VMEM(coupling.shape, F32),
            pltpu.VMEM((1, selected.shape[0]), jnp.int32),
            pltpu.SemaphoreType.DMA((4,)),
        ],
        compiler_params=pltpu.CompilerParams(vmem_limit_bytes=16 << 20),
        cost_estimate=pl.CostEstimate(flops=100_000_000, bytes_accessed=5_000_000, transcendentals=0),
        name="setup",
    )(hbm(coupling), hbm(selected[None, :]), hbm(inverses), inv_from)


def join_kernel(t0, t1, t2, t3, rhs_send, send):
    for index, tile in enumerate((t0, t1, t2, t3)):
        for half in range(2):
            send[pl.ds((2 * index + half) * NB, NB), :] = tile[half]
    send[pl.ds(CHIPS * NB, NB), :] = rhs_send[...]


def join(parts, rhs_send):
    return pl.pallas_call(
        join_kernel,
        out_shape=pltpu.VMEM(((CHIPS + 1) * NB, LANES), F32),
        in_specs=[VMEM] * 5,
        out_specs=VMEM,
        compiler_params=pltpu.CompilerParams(vmem_limit_bytes=8 << 20),
        name="join",
    )(*parts, rhs_send)


def hbm(value):
    return pltpu.with_memory_space_constraint(value, pltpu.HBM)


def apply_inverse(inv, pending):
    parts = [jnp.sum(inv[pl.ds(8 * g, 8)] * pending[None], axis=1) for g in range(NB // 8)]
    return jnp.concatenate(parts, axis=0)


def halves_of(value):
    high = value.astype(BF16)
    return high, (value - high.astype(F32)).astype(BF16)


def step_kernel(step, names, *refs):
    ref = dict(zip(names, refs))
    row, col = lax.axis_index("row"), lax.axis_index("col")
    me, core = row // 2, lax.rem(row, 2)
    chip = CHIPS - 1 - step
    active = me == chip
    inv_mine, inv_other, pend, x, send = ref["inv_mine"], ref["inv_other"], ref["pend"], ref["x"], ref["send"]
    tiles = ref["tiles"] if step else ref["tiles_out"]
    own = pl.ds(pl.multiple_of(core * NB, NB), NB)
    others = pl.ds(pl.multiple_of((1 - core) * NB, NB), NB)

    def tile(source):
        return tiles[lax.bitwise_xor(col, source)]

    def product(*terms):
        lhs = jnp.concatenate([tile(source) for source, _ in terms], axis=1)
        rhs = jnp.concatenate([value[...] for _, value in terms], axis=0)
        both = jnp.dot(lhs, rhs, preferred_element_type=F32)
        return both[:PAIR] + both[PAIR:]

    if step == 0:
        for index in range(CHIPS):
            for rows, name in ((own, "sent"), (others, "swapped")):
                high, low = halves_of(ref[name][pl.ds(index * NB, NB), :])
                tiles[index, rows, :] = high
                first = core if name == "sent" else 1 - core
                tiles[index, pl.ds(pl.multiple_of(PAIR + first * NB, NB), NB), :] = low
        pend[own, :] = ref["rhs_mine"][...]
        pend[others, :] = ref["swapped"][pl.ds(CHIPS * NB, NB), :]
    else:
        pend[...] = ref["pend_in"][...]

    @pl.when(active)
    def _():
        if step:
            near = ref["near"]
            low = jnp.concatenate([near[PAIR:, :], jnp.zeros((NB, LANES), BF16)], axis=0)
            terms = [(chip + 1, near[:PAIR, :]), (chip + 1, low)]
            if step > 1:
                terms.append((chip + 2, ref["far2"]))
            pend[...] -= product(*terms)

        def solve(odd, even):
            x_odd = apply_inverse(odd, pend[NB:, :])
            x[NB:, :] = x_odd
            high, low = halves_of(x_odd)
            send[NB:, :] = high
            parts = jnp.concatenate([high, low], axis=1)
            padded = jnp.concatenate([jnp.zeros_like(parts), parts], axis=0)
            diagonal = tile(me)
            lhs = jnp.concatenate([diagonal[:NB, :], diagonal[PAIR : PAIR + NB, :]], axis=0)
            both = jnp.dot(lhs, padded, preferred_element_type=F32)
            within = both[:NB, :LANES] + (both[:NB, LANES:] + both[NB:, :LANES])
            x_even = apply_inverse(even, pend[:NB, :] - within)
            x[:NB, :] = x_even
            high_even, low_even = halves_of(x_even)
            send[:NB, :] = high_even
            if step < CHIPS - 1:
                ahead = ref["ahead"]
                ahead[:NB, :] = high_even
                ahead[NB:PAIR, :] = high
                ahead[PAIR:, :] = low_even

        @pl.when(core == 1)
        def _():
            solve(inv_mine, inv_other)

        @pl.when(core == 0)
        def _():
            solve(inv_other, inv_mine)

    @pl.when(jnp.logical_not(active))
    def _():
        x[...] = ref["x_in"][...] if step else jnp.zeros_like(x)
        send[...] = ref["send_in"][...] if step else jnp.zeros_like(send)
        if step < CHIPS - 1:
            ref["ahead"][...] = jnp.zeros_like(ref["ahead"])
        if step > 1:
            from2, from3 = 2 * chip + 2 - me, 2 * chip + 1 - me

            @pl.when(jnp.logical_and(me < chip, from2 < CHIPS))
            def _():
                pend[...] -= product((from2, ref["far2"]))

            if "far3" in ref:

                @pl.when(jnp.logical_and(me < chip, from3 < CHIPS))
                def _():
                    pend[...] -= product((from3, ref["far3"]))

    if step == CHIPS - 1:
        ref["mine"][...] = x[own, :]
        ref["theirs"][...] = x[others, :]


def solve_step(step, operands):
    block = pltpu.VMEM((PAIR, LANES), F32)
    outs = {"send": pltpu.VMEM((PAIR, LANES), BF16)}
    scratch = {}
    if step == CHIPS - 1:
        outs["mine"] = outs["theirs"] = pltpu.VMEM((NB, LANES), F32)
        scratch["pend"] = scratch["x"] = block
    else:
        outs["pend"] = outs["x"] = block
        outs["ahead"] = pltpu.VMEM((PAIR + NB, LANES), BF16)
    if step == 0:
        outs["tiles_out"] = pltpu.VMEM((CHIPS, 2 * PAIR, LANES), BF16)
    names = list(operands) + list(outs) + list(scratch)
    call = pl.pallas_call(
        functools.partial(step_kernel, step, names),
        out_shape=tuple(outs.values()),
        in_specs=[VMEM] * len(operands),
        out_specs=(VMEM,) * len(outs),
        scratch_shapes=tuple(scratch.values()),
        compiler_params=pltpu.CompilerParams(vmem_limit_bytes=16 << 20),
        cost_estimate=pl.CostEstimate(flops=8_000_000, bytes_accessed=5_000_000, transcendentals=0),
        name="solve_step",
    )
    result = call(*operands.values())
    return dict(zip(outs, result))


BLOCK = 1536


def stack_kernel(*refs):
    parts, out = refs[:-1], refs[-1]
    size = out.shape[0] // len(parts)
    for index, part in enumerate(parts):
        out[pl.ds(index * size, size)] = part[...].reshape((size,) + out.shape[1:])


def stack(*parts):
    block = parts[0].shape[-2:]
    blocks = sum(part.size for part in parts) // (block[0] * block[1])
    return pl.pallas_call(
        stack_kernel,
        out_shape=pltpu.VMEM((blocks,) + block, parts[0].dtype),
        in_specs=[VMEM] * len(parts),
        out_specs=VMEM,
        compiler_params=pltpu.CompilerParams(vmem_limit_bytes=8 << 20),
        name="stack",
    )(*parts)


def product_kernel(pair, far1, far2, far3, pair_swap, far_swap, mine, theirs, v0, v1, v2, v3, a4, b4, a5, b5, v6, v7, out, slab, x_all):
    row, col = lax.axis_index("row"), lax.axis_index("col")
    core, xlo, y = lax.rem(row, 2), lax.rem(row // 2, 2), row // 4

    @pl.when(pl.program_id(0) == 0)
    def _():
        for mask, left in enumerate((pair, far1, far2, far3)):
            for cross in range(2):
                index = lax.bitwise_xor(2 * lax.bitwise_xor(y, mask) + xlo, cross)
                slot = pl.ds(pl.multiple_of(lax.bitwise_xor(col, index) * PAIR, PAIR), PAIR)
                x_all[slot, core_lanes(core)] = left[cross]
                right = far_swap[2 * mask - 2 + cross] if mask else pair_swap[cross]
                x_all[slot, core_lanes(1 - core)] = right
        slab[:, core_lanes(core)] = mine[...]
        slab[:, core_lanes(1 - core)] = theirs[...]

    first = pl.program_id(0) < pl.num_programs(0) // 2
    half = pl.num_programs(0) // 2
    rows = pl.ds(pl.multiple_of(pl.program_id(0) * BLOCK, BLOCK), BLOCK)
    part = pl.ds(pl.multiple_of(lax.rem(pl.program_id(0), half) * BLOCK, BLOCK), BLOCK)
    v4 = jnp.where(first, a4[part, :], b4[part, :])
    v5 = jnp.where(first, a5[part, :], b5[part, :])
    lhs = jnp.concatenate([v0[rows, :], v1[rows, :], v2[rows, :], v3[rows, :], v4, v5, v6[rows, :], v7[rows, :]], axis=1)
    out[...] = jnp.dot(lhs, x_all[...], preferred_element_type=F32).astype(out.dtype)


def back_transform(factors, slabs, shards):
    rows = shards[0].shape[0]
    half = rows // BLOCK // 2
    block = pl.BlockSpec((BLOCK, LANES), lambda i: (i, 0))
    low = pl.BlockSpec((BLOCK, LANES), lambda i: (jnp.minimum(i, half - 1), 0))
    high = pl.BlockSpec((BLOCK, LANES), lambda i: (jnp.maximum(i - half, 0), 0))
    return pl.pallas_call(
        product_kernel,
        grid=(rows // BLOCK,),
        out_shape=(
            jax.ShapeDtypeStruct((rows, 2 * LANES), BF16),
            jax.ShapeDtypeStruct((NB, 2 * LANES), F32),
        ),
        in_specs=[VMEM] * 18,
        out_specs=(pl.BlockSpec((BLOCK, 2 * LANES), lambda i: (i, 0)), VMEM),
        scratch_shapes=[pltpu.VMEM((CHIPS * PAIR, 2 * LANES), BF16)],
        compiler_params=pltpu.CompilerParams(vmem_limit_bytes=24 << 20),
        cost_estimate=pl.CostEstimate(flops=2 * rows * 1024 * 256, bytes_accessed=8_000_000, transcendentals=0),
        name="back_transform",
    )(*factors, *slabs, *shards)


def per_device(schur_rows, inverses, coupling, selected, schur_basis):
    def col_flip(value, mask):
        return lax.ppermute(value, "col", flip(CHIPS, mask))

    def row_move(value, pairs):
        return lax.ppermute(value, "row", pairs)

    def row_flip(value, mask):
        return row_move(value, flip(2 * CHIPS, mask))

    t0 = stack(schur_rows, col_flip(schur_rows, 1))
    parts = [t0] + [col_flip(t0, mask) for mask in (2, 4, 6)]
    inv_from = row_flip(inverses, 1)

    v = {0: schur_basis, 1: col_flip(schur_basis, 1)}
    v[2], v[6] = col_flip(schur_basis, 2), col_flip(schur_basis, 6)
    split = schur_basis.shape[0] // 2

    inv_mine, inv_other, rhs_mine, rhs_send = setup(coupling, selected, inverses, inv_from)
    sent = join(parts, rhs_send)
    swapped = row_flip(sent, 1)
    kept = {"inv_mine": inv_mine, "inv_other": inv_other}
    state = solve_step(0, {"rhs_mine": rhs_mine, "sent": sent, "swapped": swapped, **kept})
    kept["tiles"] = state["tiles_out"]
    late = {}
    for step in range(1, CHIPS):
        near, far2, far3 = moves(step - 1)
        operands = {"pend_in": state["pend"], "x_in": state["x"], "send_in": state["send"]}
        operands["near"] = row_move(state["ahead"], near)
        operands.update(late)
        late = {name: row_move(state["send"], pairs) for name, pairs in (("far2", far2), ("far3", far3)) if pairs}
        state = solve_step(step, {**operands, **kept})
        if step == 1:
            v[1], _ = lax.optimization_barrier((v[1], state["x"]))
            v[3], v[7] = col_flip(v[1], 2), col_flip(v[1], 6)
        if step == 3:
            v[2], v[6], _ = lax.optimization_barrier((v[2], v[6], state["x"]))
            a4, b4 = col_flip(v[6][:split], 2), col_flip(v[2][split:], 6)
        if step == 6:
            v[3], v[7], _ = lax.optimization_barrier((v[3], v[7], state["x"]))
            a5, b5 = col_flip(v[7][:split], 2), col_flip(v[3][split:], 6)

    factor = state["send"]
    pair = stack(factor, row_flip(factor, 2))
    far = [row_flip(pair, 4 * mask) for mask in (1, 2, 3)]
    factors = (pair, *far, row_flip(pair, 1), row_flip(stack(*far), 1))
    slabs = (state["mine"], row_flip(state["theirs"], 1))
    return back_transform(factors, slabs, (v[0], v[1], v[2], v[3], a4, b4, a5, b5, v[6], v[7]))


def solution(mesh):
    in_specs = (P("row", "col"), P("row", None, "col"), P("row", None), P("col"), P("row", "col"))
    out_specs = (P("row", "col"), P("row", "col"))
    return jax.shard_map(per_device, mesh=mesh, in_specs=in_specs, out_specs=out_specs, check_vma=False)
```

```python
import functools

import jax
import jax.numpy as jnp
from jax import lax
from jax.experimental import pallas as pl
from jax.experimental.pallas import tpu as pltpu
from jax.sharding import PartitionSpec as P


NB = 64
LANES = 128
PAIR = 2 * NB
PLAIN_HOPS = 3
CHIPS = 8
F32 = jnp.float32
BF16 = jnp.bfloat16


VMEM = pl.BlockSpec(memory_space=pltpu.VMEM)
HBM = pl.BlockSpec(memory_space=pltpu.MemorySpace.HBM)


def flip(values, mask):
    return [(i, i ^ mask) for i in range(values)]


def moves(step):
    chip = CHIPS - 1 - step
    result = []
    for least in (1, 2, 3):
        chips = [(chip + k, chip - least - k) for k in range(CHIPS if least > 1 else 1)]
        chips = [(a, b) for a, b in chips if a < CHIPS and b >= 0]
        result.append([(2 * a + core, 2 * b + core) for a, b in chips for core in (0, 1)])
    return result


def core_lanes(core):
    return pl.ds(pl.multiple_of(core * LANES, LANES), LANES)


def setup_kernel(candidates_from, selected_from, inv, inv_from, inv_mine, inv_other, rhs_mine, rhs_send, coupling, selected, sem):
    core = lax.rem(lax.axis_index("row"), 2)
    copies = [
        pltpu.make_async_copy(candidates_from, coupling, sem.at[0]),
        pltpu.make_async_copy(selected_from, selected, sem.at[1]),
        pltpu.make_async_copy(inv.at[:, :, core_lanes(core)], inv_mine, sem.at[2]),
        pltpu.make_async_copy(inv_from.at[:, :, core_lanes(core)], inv_other, sem.at[3]),
    ]
    for copy in copies:
        copy.start()
    copies[0].wait()
    copies[1].wait()
    candidates, columns = coupling.shape[1], selected.shape[1]
    piece = 256
    total = jnp.zeros((3 * NB, columns), F32)
    for first in range(0, candidates, piece):
        part = coupling[:, first : first + piece]
        high = part.astype(BF16)
        rest = part - high.astype(F32)
        middle = rest.astype(BF16)
        low = (rest - middle.astype(F32)).astype(BF16)
        index = lax.broadcasted_iota(jnp.int32, (piece, columns), 0) + first
        chosen = jnp.where(index == selected[...], 1.0, 0.0).astype(BF16)
        total += jnp.dot(jnp.concatenate([high, middle, low], axis=0), chosen, preferred_element_type=F32)
    rhs = -(total[:NB] + total[NB : 2 * NB] + total[2 * NB :])
    left, right = rhs[:, :LANES], rhs[:, LANES:]
    rhs_mine[...] = jnp.where(core == 0, left, right)
    rhs_send[...] = jnp.where(core == 0, right, left)
    copies[2].wait()
    copies[3].wait()


def setup(coupling, selected, inverses, inv_from):
    half = pltpu.VMEM((NB, NB, LANES), F32)
    side = pltpu.VMEM((NB, LANES), F32)
    return pl.pallas_call(
        setup_kernel,
        out_shape=(half, half, side, side),
        in_specs=[HBM] * 4,
        out_specs=(VMEM,) * 4,
        scratch_shapes=[
            pltpu.VMEM(coupling.shape, F32),
            pltpu.VMEM((1, selected.shape[0]), jnp.int32),
            pltpu.SemaphoreType.DMA((4,)),
        ],
        compiler_params=pltpu.CompilerParams(vmem_limit_bytes=16 << 20),
        cost_estimate=pl.CostEstimate(flops=100_000_000, bytes_accessed=5_000_000, transcendentals=0),
        name="setup",
    )(hbm(coupling), hbm(selected[None, :]), hbm(inverses), inv_from)


def join_kernel(t0, t1, t2, t3, rhs_send, send):
    for index, tile in enumerate((t0, t1, t2, t3)):
        for half in range(2):
            send[pl.ds((2 * index + half) * NB, NB), :] = tile[half]
    send[pl.ds(CHIPS * NB, NB), :] = rhs_send[...]


def join(parts, rhs_send):
    return pl.pallas_call(
        join_kernel,
        out_shape=pltpu.VMEM(((CHIPS + 1) * NB, LANES), F32),
        in_specs=[VMEM] * 5,
        out_specs=VMEM,
        compiler_params=pltpu.CompilerParams(vmem_limit_bytes=8 << 20),
        name="join",
    )(*parts, rhs_send)


def hbm(value):
    return pltpu.with_memory_space_constraint(value, pltpu.HBM)


def apply_inverse(inv, pending):
    parts = [jnp.sum(inv[pl.ds(8 * g, 8)] * pending[None], axis=1) for g in range(NB // 8)]
    return jnp.concatenate(parts, axis=0)


def halves_of(value):
    high = value.astype(BF16)
    return high, (value - high.astype(F32)).astype(BF16)


def step_kernel(step, names, *refs):
    ref = dict(zip(names, refs))
    row, col = lax.axis_index("row"), lax.axis_index("col")
    me, core = row // 2, lax.rem(row, 2)
    chip = CHIPS - 1 - step
    active = me == chip
    inv_mine, inv_other, pend, x, send = ref["inv_mine"], ref["inv_other"], ref["pend"], ref["x"], ref["send"]
    tiles = ref["tiles"] if step else ref["tiles_out"]
    own = pl.ds(pl.multiple_of(core * NB, NB), NB)
    others = pl.ds(pl.multiple_of((1 - core) * NB, NB), NB)

    def tile(source):
        return tiles[lax.bitwise_xor(col, source)]

    def product(*terms):
        lhs = jnp.concatenate([tile(source) for source, _ in terms], axis=1)
        rhs = jnp.concatenate([value[...] for _, value in terms], axis=0)
        both = jnp.dot(lhs, rhs, preferred_element_type=F32)
        return both[:PAIR] + both[PAIR:]

    if step == 0:
        for index in range(CHIPS):
            for rows, name in ((own, "sent"), (others, "swapped")):
                high, low = halves_of(ref[name][pl.ds(index * NB, NB), :])
                tiles[index, rows, :] = high
                first = core if name == "sent" else 1 - core
                tiles[index, pl.ds(pl.multiple_of(PAIR + first * NB, NB), NB), :] = low
        pend[own, :] = ref["rhs_mine"][...]
        pend[others, :] = ref["swapped"][pl.ds(CHIPS * NB, NB), :]
    else:
        pend[...] = ref["pend_in"][...]

    @pl.when(active)
    def _():
        if step:
            near = ref["near"]
            terms = [(chip + 1, near[:PAIR, :])]
            if step > PLAIN_HOPS:
                low = jnp.concatenate([near[PAIR:, :], jnp.zeros((NB, LANES), BF16)], axis=0)
                terms.append((chip + 1, low))
            if step > 1:
                terms.append((chip + 2, ref["far2"]))
            pend[...] -= product(*terms)

        def solve(odd, even):
            x_odd = apply_inverse(odd, pend[NB:, :])
            x[NB:, :] = x_odd
            high, low = halves_of(x_odd)
            send[NB:, :] = high
            parts = jnp.concatenate([high, low], axis=1)
            padded = jnp.concatenate([jnp.zeros_like(parts), parts], axis=0)
            diagonal = tile(me)
            lhs = jnp.concatenate([diagonal[:NB, :], diagonal[PAIR : PAIR + NB, :]], axis=0)
            both = jnp.dot(lhs, padded, preferred_element_type=F32)
            within = both[:NB, :LANES] + (both[:NB, LANES:] + both[NB:, :LANES])
            x_even = apply_inverse(even, pend[:NB, :] - within)
            x[:NB, :] = x_even
            high_even, low_even = halves_of(x_even)
            send[:NB, :] = high_even
            if PLAIN_HOPS <= step < CHIPS - 1:
                ahead = ref["ahead"]
                ahead[:NB, :] = high_even
                ahead[NB:PAIR, :] = high
                ahead[PAIR:, :] = low_even

        @pl.when(core == 1)
        def _():
            solve(inv_mine, inv_other)

        @pl.when(core == 0)
        def _():
            solve(inv_other, inv_mine)

    @pl.when(jnp.logical_not(active))
    def _():
        x[...] = ref["x_in"][...] if step else jnp.zeros_like(x)
        send[...] = ref["send_in"][...] if step else jnp.zeros_like(send)
        if PLAIN_HOPS <= step < CHIPS - 1:
            ref["ahead"][...] = jnp.zeros_like(ref["ahead"])
        if step > 1:
            from2, from3 = 2 * chip + 2 - me, 2 * chip + 1 - me

            @pl.when(jnp.logical_and(me < chip, from2 < CHIPS))
            def _():
                pend[...] -= product((from2, ref["far2"]))

            if "far3" in ref:

                @pl.when(jnp.logical_and(me < chip, from3 < CHIPS))
                def _():
                    pend[...] -= product((from3, ref["far3"]))

    if step == CHIPS - 1:
        ref["mine"][...] = x[own, :]
        ref["theirs"][...] = x[others, :]


def solve_step(step, operands):
    block = pltpu.VMEM((PAIR, LANES), F32)
    outs = {"send": pltpu.VMEM((PAIR, LANES), BF16)}
    scratch = {}
    if step == CHIPS - 1:
        outs["mine"] = outs["theirs"] = pltpu.VMEM((NB, LANES), F32)
        scratch["pend"] = scratch["x"] = block
    else:
        outs["pend"] = outs["x"] = block
        if step >= PLAIN_HOPS:
            outs["ahead"] = pltpu.VMEM((PAIR + NB, LANES), BF16)
    if step == 0:
        outs["tiles_out"] = pltpu.VMEM((CHIPS, 2 * PAIR, LANES), BF16)
    names = list(operands) + list(outs) + list(scratch)
    call = pl.pallas_call(
        functools.partial(step_kernel, step, names),
        out_shape=tuple(outs.values()),
        in_specs=[VMEM] * len(operands),
        out_specs=(VMEM,) * len(outs),
        scratch_shapes=tuple(scratch.values()),
        compiler_params=pltpu.CompilerParams(vmem_limit_bytes=16 << 20),
        cost_estimate=pl.CostEstimate(flops=8_000_000, bytes_accessed=5_000_000, transcendentals=0),
        name="solve_step",
    )
    result = call(*operands.values())
    return dict(zip(outs, result))


BLOCK = 1536


def stack_kernel(*refs):
    parts, out = refs[:-1], refs[-1]
    size = out.shape[0] // len(parts)
    for index, part in enumerate(parts):
        out[pl.ds(index * size, size)] = part[...].reshape((size,) + out.shape[1:])


def stack(*parts):
    block = parts[0].shape[-2:]
    blocks = sum(part.size for part in parts) // (block[0] * block[1])
    return pl.pallas_call(
        stack_kernel,
        out_shape=pltpu.VMEM((blocks,) + block, parts[0].dtype),
        in_specs=[VMEM] * len(parts),
        out_specs=VMEM,
        compiler_params=pltpu.CompilerParams(vmem_limit_bytes=8 << 20),
        name="stack",
    )(*parts)


def product_kernel(pair, far1, far2, far3, pair_swap, far_swap, mine, theirs, v0, v1, v2, v3, a4, b4, a5, b5, v6, v7, out, slab, x_all):
    row, col = lax.axis_index("row"), lax.axis_index("col")
    core, xlo, y = lax.rem(row, 2), lax.rem(row // 2, 2), row // 4

    @pl.when(pl.program_id(0) == 0)
    def _():
        for mask, left in enumerate((pair, far1, far2, far3)):
            for cross in range(2):
                index = lax.bitwise_xor(2 * lax.bitwise_xor(y, mask) + xlo, cross)
                slot = pl.ds(pl.multiple_of(lax.bitwise_xor(col, index) * PAIR, PAIR), PAIR)
                x_all[slot, core_lanes(core)] = left[cross]
                right = far_swap[2 * mask - 2 + cross] if mask else pair_swap[cross]
                x_all[slot, core_lanes(1 - core)] = right
        slab[:, core_lanes(core)] = mine[...]
        slab[:, core_lanes(1 - core)] = theirs[...]

    first = pl.program_id(0) < pl.num_programs(0) // 2
    half = pl.num_programs(0) // 2
    rows = pl.ds(pl.multiple_of(pl.program_id(0) * BLOCK, BLOCK), BLOCK)
    part = pl.ds(pl.multiple_of(lax.rem(pl.program_id(0), half) * BLOCK, BLOCK), BLOCK)
    v4 = jnp.where(first, a4[part, :], b4[part, :])
    v5 = jnp.where(first, a5[part, :], b5[part, :])
    lhs = jnp.concatenate([v0[rows, :], v1[rows, :], v2[rows, :], v3[rows, :], v4, v5, v6[rows, :], v7[rows, :]], axis=1)
    out[...] = jnp.dot(lhs, x_all[...], preferred_element_type=F32).astype(out.dtype)


def back_transform(factors, slabs, shards):
    rows = shards[0].shape[0]
    half = rows // BLOCK // 2
    block = pl.BlockSpec((BLOCK, LANES), lambda i: (i, 0))
    low = pl.BlockSpec((BLOCK, LANES), lambda i: (jnp.minimum(i, half - 1), 0))
    high = pl.BlockSpec((BLOCK, LANES), lambda i: (jnp.maximum(i - half, 0), 0))
    return pl.pallas_call(
        product_kernel,
        grid=(rows // BLOCK,),
        out_shape=(
            jax.ShapeDtypeStruct((rows, 2 * LANES), BF16),
            jax.ShapeDtypeStruct((NB, 2 * LANES), F32),
        ),
        in_specs=[VMEM] * 18,
        out_specs=(pl.BlockSpec((BLOCK, 2 * LANES), lambda i: (i, 0)), VMEM),
        scratch_shapes=[pltpu.VMEM((CHIPS * PAIR, 2 * LANES), BF16)],
        compiler_params=pltpu.CompilerParams(vmem_limit_bytes=24 << 20),
        cost_estimate=pl.CostEstimate(flops=2 * rows * 1024 * 256, bytes_accessed=8_000_000, transcendentals=0),
        name="back_transform",
    )(*factors, *slabs, *shards)


def per_device(schur_rows, inverses, coupling, selected, schur_basis):
    def col_flip(value, mask):
        return lax.ppermute(value, "col", flip(CHIPS, mask))

    def row_move(value, pairs):
        return lax.ppermute(value, "row", pairs)

    def row_flip(value, mask):
        return row_move(value, flip(2 * CHIPS, mask))

    t0 = stack(schur_rows, col_flip(schur_rows, 1))
    parts = [t0] + [col_flip(t0, mask) for mask in (2, 4, 6)]
    inv_from = row_flip(inverses, 1)

    v = {0: schur_basis, 1: col_flip(schur_basis, 1)}
    v[2], v[6] = col_flip(schur_basis, 2), col_flip(schur_basis, 6)
    split = schur_basis.shape[0] // 2

    inv_mine, inv_other, rhs_mine, rhs_send = setup(coupling, selected, inverses, inv_from)
    sent = join(parts, rhs_send)
    swapped = row_flip(sent, 1)
    kept = {"inv_mine": inv_mine, "inv_other": inv_other}
    state = solve_step(0, {"rhs_mine": rhs_mine, "sent": sent, "swapped": swapped, **kept})
    kept["tiles"] = state["tiles_out"]
    late = {}
    for step in range(1, CHIPS):
        near, far2, far3 = moves(step - 1)
        operands = {"pend_in": state["pend"], "x_in": state["x"], "send_in": state["send"]}
        operands["near"] = row_move(state["ahead" if step > PLAIN_HOPS else "send"], near)
        operands.update(late)
        late = {name: row_move(state["send"], pairs) for name, pairs in (("far2", far2), ("far3", far3)) if pairs}
        state = solve_step(step, {**operands, **kept})
        if step == 1:
            v[1], _ = lax.optimization_barrier((v[1], state["x"]))
            v[3], v[7] = col_flip(v[1], 2), col_flip(v[1], 6)
        if step == 3:
            v[2], v[6], _ = lax.optimization_barrier((v[2], v[6], state["x"]))
            a4, b4 = col_flip(v[6][:split], 2), col_flip(v[2][split:], 6)
        if step == 6:
            v[3], v[7], _ = lax.optimization_barrier((v[3], v[7], state["x"]))
            a5, b5 = col_flip(v[7][:split], 2), col_flip(v[3][split:], 6)

    factor = state["send"]
    pair = stack(factor, row_flip(factor, 2))
    far = [row_flip(pair, 4 * mask) for mask in (1, 2, 3)]
    factors = (pair, *far, row_flip(pair, 1), row_flip(stack(*far), 1))
    slabs = (state["mine"], row_flip(state["theirs"], 1))
    return back_transform(factors, slabs, (v[0], v[1], v[2], v[3], a4, b4, a5, b5, v[6], v[7]))


def solution(mesh):
    in_specs = (P("row", "col"), P("row", None, "col"), P("row", None), P("col"), P("row", "col"))
    out_specs = (P("row", "col"), P("row", "col"))
    return jax.shard_map(per_device, mesh=mesh, in_specs=in_specs, out_specs=out_specs, check_vma=False)
```
